256 devices in a mesh: rep: 4 (over x), table: 64 (over z, y, core).
Axes of the slice: x: 4, y: 4, z: 8, core: 2. Of those that a mesh axis runs over, the one named last changes fastest.
Arguments:
- cold_table: float32 [65536, 400], P('table'), may hold values from -3 to 3
- cold_state: float32 [65536], P('table'), may hold values from 0.05 to 1
- hot_table: float32 [8192, 400], P('table'), may hold values from -3 to 3
- hot_state: float32 [8192], P('table'), may hold values from 0.05 to 1
- relations: float32 [512, 400], replicated, may hold values from -2.5 to 2.5
- head_owner: int32 [131072, 1], P(('rep', 'table')), may hold values from 0 to 63; in each aligned block of 512 rows (0 to 511, 512 to 1023, ...) at most 16 rows name the same one
- head_row: int32 [131072], P(('rep', 'table')), may hold values from 0 to 1023
- edge_rel: int32 [131072], P(('rep', 'table')), may hold values from 0 to 511
- edge_tail: int32 [131072], P(('rep', 'table')), may hold values from 0 to 8191, as said below
- neg_ids: int32 [4, 512], P('rep', 'table'), may hold values from 0 to 1023
Outputs:
- new_cold_table: float32 [65536, 400], P('table')
- new_cold_state: float32 [65536], P('table')
- new_hot_table: float32 [8192, 400], P('table')
- new_hot_state: float32 [8192], P('table')
The draws below stay inside these ranges and needn't reach their ends.
Inputs may be any that keep to these rules, and one draw needn't show every extreme that they name: `head_owner`: among the edges of one device (aligned blocks of 512), no owner is named more than 16 times. `neg_ids`: column j names a row of the cold rows of table index j // 8. `edge_tail`: among the edges of one device (aligned blocks of 512), the tails that lie in one aligned block of 128 hot rows are at most 32 distinct rows, and in some such block exactly 32.
All inputs are finite; a program needn't handle non-finite values.
Results may differ from the reference program's by a relative error of at most 0.00045.
The reference program's roundings to bfloat16 on the way count: a program that leaves them out, or rounds other values in their place, can miss the bound.
Values may be sent and summed in bfloat16 or wider, within the bound.
No kernel may reach another device: no remote copies, remote signals or barrier semaphores. Data moves between devices by JAX's collectives and lax.ppermute only.
A program may use at most 128 MiB of HBM per device.

```python
import math
import jax
import jax.numpy as jnp
import numpy as np
from jax import lax

D = 400
REL = 512
HOT_DEV = 128
TAIL_CAP = 32
COLD_DEV = 1024
EDGES_DEV = 512
NEG_DEV = 8
CAP = 16
HOT = 8192
COLD = 65536
NEG = 512
EDGES = 131072
N_REP = 4
N_TABLE = 64


def draw_edge_tail(key, part):
    blocks = EDGES // EDGES_DEV
    owner_count = HOT // HOT_DEV
    key_perm, key_owner, key_slot, key_full = jax.random.split(jax.random.fold_in(key, 7), 4)
    perm_keys = jax.random.split(key_perm, blocks * owner_count)
    chosen = jax.vmap(lambda single: jax.random.permutation(single, HOT_DEV)[:TAIL_CAP])(perm_keys)
    chosen = chosen.reshape(blocks, owner_count, TAIL_CAP).astype(jnp.int32)
    owner_ids = jax.random.randint(key_owner, (blocks, EDGES_DEV), 0, owner_count, dtype=jnp.int32)
    slot_ids = jax.random.randint(key_slot, (blocks, EDGES_DEV), 0, TAIL_CAP, dtype=jnp.int32)
    full_owner = jax.random.randint(key_full, (blocks, 1), 0, owner_count, dtype=jnp.int32)
    position = jnp.arange(EDGES_DEV, dtype=jnp.int32)[None, :]
    leading = position < TAIL_CAP
    owner_ids = jnp.where(leading, full_owner, owner_ids)
    slot_ids = jnp.where(leading, jnp.minimum(position, TAIL_CAP - 1), slot_ids)
    block_ids = jnp.arange(blocks, dtype=jnp.int32)[:, None]
    picked = chosen[block_ids, owner_ids, slot_ids]
    return (owner_ids * HOT_DEV + picked).reshape(EDGES).astype(jnp.int32)


def place_ends(entries, rng, smallest, largest):
    dims = entries.shape
    place = [jax.random.randint(jax.random.fold_in(rng, axis), (), 0, dims[axis]) for axis in range(len(dims))]
    entries = entries.at[tuple(place)].set(smallest)
    longest = dims.index(max(dims))
    place[longest] = (place[longest] + 1) % dims[longest]
    return entries.at[tuple(place)].set(largest)


def block_levels(stream_key, dims, shards, least, high):
    loudness = 1.0
    for dim, parts in shards:
        heights = jax.random.uniform(jax.random.fold_in(jax.random.fold_in(stream_key, 6), dim), (parts,), jnp.float32, least / len(shards), high / len(shards))
        loudness = loudness * jnp.repeat(jnp.exp(heights), dims[dim] // parts).reshape((-1,) + (1,) * (len(dims) - 1 - dim))
    return loudness


def shared_out(stream_key, own, number, rows, count, top, most, skew):
    ranking = jax.random.permutation(stream_key, count)
    heavy_load, ordinary = portions_of(count, rows * top, most, skew, True), portions_of(count, rows * top, most, skew, False)
    places = jnp.arange(count)

    def named(lengths, offset_by):
        used = int((lengths > 0).sum())
        fixed = max(1, used // 4)
        moved = fixed + (places - fixed + offset_by * (used - fixed)) % max(1, count - fixed)
        return jnp.zeros((count,), jnp.int32).at[ranking[jnp.where(places < fixed, places, moved)]].set(jnp.asarray(lengths, jnp.int32))

    lengths = jnp.where(number % 4 == 0, named(heavy_load, number // 4), named(ordinary, number - number // 4 - 1))
    mixed = jax.random.permutation(jax.random.fold_in(own, 3), count)
    giver, receiver = mixed[0:count // 2 * 2:2], mixed[1:count // 2 * 2:2]
    room = jnp.minimum(lengths[giver] - 1, most - lengths[receiver]) // 2
    room = jnp.where((giver == ranking[0]) | (receiver == ranking[0]) | (lengths[receiver] == 0), 0, jnp.maximum(room, 0))
    moved = jax.random.randint(jax.random.fold_in(own, 4), (count // 2,), 0, 1 << 20) % (room + 1)
    lengths = lengths.at[giver].add(-moved).at[receiver].add(moved)
    items = jnp.searchsorted(jnp.cumsum(lengths), jnp.arange(rows * top), side="right").astype(jnp.int32)
    listing = items.reshape(top, rows).T
    listing = listing[jax.random.permutation(jax.random.fold_in(own, 1), rows)]
    offset_by = jax.random.randint(jax.random.fold_in(own, 2), (rows, 1), 0, top)
    return jnp.take_along_axis(listing, (jnp.arange(top)[None, :] + offset_by) % top, axis=1)


def portions_of(count, total, most, lean, full):
    portions = [(1 << 20) // math.isqrt(rank ** lean) + 1 for rank in range(1, count + 1)]
    largest = most if full else min(most, max(-(-total // count), total * portions[0] // sum(portions)))
    least = 1 if total - largest >= count - 1 else 0
    counts, spare = [largest] + [least] * (count - 1), total - largest - least * (count - 1)
    while spare > 0:
        free = [i for i in range(1, count) if counts[i] < largest] or [i for i in range(1, count) if counts[i] < most]
        pool, left = sum([portions[i] for i in free]), spare
        for i in free:
            more = min(most - counts[i], max(1, left * portions[i] // pool), spare)
            counts[i] = counts[i] + more
            spare = spare - more
    return np.array(counts)


def scatter_about(key, extent, scale, reach, pieces=(), kind=jnp.bfloat16):
    entries = scale * jax.random.normal(key, extent, jnp.float32)
    if pieces:
        entries = entries * block_levels(key, extent, pieces, -0.22, 0.18)
    return jnp.clip(entries, -reach, reach).astype(kind)


def setup_inputs(seed: int = 0) -> dict:
    arg_keys = jax.random.split(jax.random.key(seed), 11)
    cold_table = scatter_about(arg_keys[0], (COLD, D), 0.5, 3.0, ((0, 64),), jnp.float32)
    cold_state = jnp.clip(jnp.exp(math.log(1.0) - 2.9957323 * jax.random.uniform(arg_keys[1], (COLD,), jnp.float32) ** block_levels(arg_keys[1], (COLD,), ((0, 64),), -0.2, 0.2)), 0.05, 1.0)
    hot_table = scatter_about(arg_keys[2], (HOT, D), 0.5, 3.0, ((0, 64),), jnp.float32)
    hot_state = jnp.clip(jnp.exp(math.log(1.0) - 2.9957323 * jax.random.uniform(arg_keys[3], (HOT,), jnp.float32) ** block_levels(arg_keys[3], (HOT,), ((0, 64),), -0.2, 0.2)), 0.05, 1.0)
    relations = scatter_about(arg_keys[4], (REL, D), 0.2, 2.5, (), jnp.float32)
    head_owner_keys = jax.random.split(jax.random.fold_in(arg_keys[5], 1), EDGES // EDGES_DEV)
    head_owner_turns = jax.random.permutation(jax.random.fold_in(arg_keys[5], 3), EDGES // EDGES_DEV)
    head_owner = jax.vmap(lambda own, number: shared_out(jax.random.fold_in(arg_keys[5], 2), own, number, EDGES_DEV, N_TABLE, 1, CAP, 2))(head_owner_keys, head_owner_turns).reshape((EDGES, 1))
    head_row = place_ends(jax.random.randint(arg_keys[6], (EDGES,), 0, COLD_DEV), jax.random.fold_in(arg_keys[6], 1), 0, COLD_DEV - 1).astype(jnp.int32)
    edge_rel = place_ends(jax.random.randint(arg_keys[7], (EDGES,), 0, REL), jax.random.fold_in(arg_keys[7], 1), 0, REL - 1).astype(jnp.int32)
    edge_tail = draw_edge_tail(jax.random.fold_in(arg_keys[10], 71), 0)
    neg_ids = place_ends(jax.random.randint(arg_keys[9], (N_REP, NEG), 0, COLD_DEV), jax.random.fold_in(arg_keys[9], 1), 0, COLD_DEV - 1).astype(jnp.int32)
    return {"cold_table": cold_table, "cold_state": cold_state, "hot_table": hot_table, "hot_state": hot_state, "relations": relations, "head_owner": head_owner, "head_row": head_row, "edge_rel": edge_rel, "edge_tail": edge_tail, "neg_ids": neg_ids}


learn_rate = 0.5

def with_relation(relation, vector):
    half_width = vector.shape[1] // 2
    v_re, v_im = (vector[:, :half_width], vector[:, half_width:])
    r_re, r_im = (relation[:, :half_width], relation[:, half_width:])
    return jnp.concatenate([v_re * r_re - v_im * r_im, v_re * r_im + v_im * r_re], axis=1)

def against_relation(relation, vector):
    half_width = vector.shape[1] // 2
    v_re, v_im = (vector[:, :half_width], vector[:, half_width:])
    r_re, r_im = (relation[:, :half_width], relation[:, half_width:])
    return jnp.concatenate([r_re * v_re + r_im * v_im, r_re * v_im - r_im * v_re], axis=1)

def edge_terms(head_vec, relation, tail_vec, negatives, live_mask):
    head_f = head_vec.astype(jnp.float32)
    tail_f = tail_vec.astype(jnp.float32)
    queries = with_relation(relation, head_f)
    probes = against_relation(relation, tail_f)
    positive = lax.optimization_barrier(jnp.sum(queries * tail_f, axis=1))
    query_b = queries.astype(jnp.bfloat16)
    probe_b = probes.astype(jnp.bfloat16)
    tail_scores = jnp.dot(query_b, negatives.T, preferred_element_type=jnp.float32)
    head_scores = jnp.dot(probe_b, negatives.T, preferred_element_type=jnp.float32)
    pos_weight = -jax.nn.sigmoid(-positive) * live_mask
    tail_weight = (jax.nn.sigmoid(tail_scores) * live_mask[:, None]).astype(jnp.bfloat16)
    head_weight = (jax.nn.sigmoid(head_scores) * live_mask[:, None]).astype(jnp.bfloat16)
    tail_mix = jnp.dot(tail_weight, negatives, preferred_element_type=jnp.float32)
    head_mix = jnp.dot(head_weight, negatives, preferred_element_type=jnp.float32)
    head_grad = against_relation(relation, pos_weight[:, None] * tail_f + tail_mix).astype(jnp.bfloat16)
    tail_grad = with_relation(relation, pos_weight[:, None] * head_f + head_mix)
    neg_grad = jnp.dot(tail_weight.T, query_b, preferred_element_type=jnp.float32) + jnp.dot(head_weight.T, probe_b, preferred_element_type=jnp.float32)
    return (head_grad, tail_grad, neg_grad)

def adagrad(weights, state, grad):
    new_state = state + lax.optimization_barrier(jnp.mean(grad * grad, axis=1))
    return (weights - learn_rate * grad / jnp.sqrt(new_state)[:, None], new_state)

def reference(cold_table, cold_state, hot_table, hot_state, relations, head_owner, head_row, edge_rel, edge_tail, neg_ids):
    cold_bf = cold_table.astype(jnp.bfloat16)
    hot_bf = hot_table.astype(jnp.bfloat16)
    head_ids = (head_owner[:, 0] * COLD_DEV + head_row).astype(jnp.int32)
    shard_base = (jnp.arange(NEG, dtype=jnp.int32) // NEG_DEV * COLD_DEV).astype(jnp.int32)
    live_mask = jnp.ones((EDGES_DEV,), jnp.float32)

    def accumulate(totals, block_idx):
        cold_grad, hot_grad = totals
        replica = block_idx // N_TABLE
        start = (block_idx * EDGES_DEV).astype(jnp.int32)
        heads = lax.dynamic_slice_in_dim(head_ids, start, EDGES_DEV)
        rel_ids = lax.dynamic_slice_in_dim(edge_rel, start, EDGES_DEV)
        tails = lax.dynamic_slice_in_dim(edge_tail, start, EDGES_DEV)
        neg_rows = (lax.dynamic_index_in_dim(neg_ids, replica, 0, keepdims=False) + shard_base).astype(jnp.int32)
        negatives = cold_bf[neg_rows]
        head_grad, tail_grad, neg_grad = edge_terms(cold_bf[heads], relations[rel_ids], hot_bf[tails], negatives, live_mask)
        cold_grad = cold_grad.at[heads].add(head_grad.astype(jnp.float32))
        cold_grad = cold_grad.at[neg_rows].add(neg_grad)
        hot_grad = hot_grad.at[tails].add(tail_grad)
        return ((cold_grad, hot_grad), None)
    start_totals = (jnp.zeros(cold_table.shape, jnp.float32), jnp.zeros(hot_table.shape, jnp.float32))
    (cold_grad, hot_grad), unused = lax.scan(accumulate, start_totals, jnp.arange(N_REP * N_TABLE, dtype=jnp.int32))
    new_cold_table, new_cold_state = adagrad(cold_table, cold_state, cold_grad)
    new_hot_table, new_hot_state = adagrad(hot_table, hot_state, hot_grad)
    return (new_cold_table, new_cold_state, new_hot_table, new_hot_state)
```

```python
import functools
import jax
import jax.numpy as jnp
from jax import lax
from jax.experimental import pallas as pl
from jax.experimental.pallas import tpu as pltpu
from jax.sharding import PartitionSpec as P

learn_rate = 0.5
HEAD_CAP = 16
TAIL_CAP = 32
GROUP = 8
HALF = 256
FULL = 2 * HALF

BF = jnp.bfloat16
F16 = jnp.float16
F32 = jnp.float32
I32 = jnp.int32


def dot(a, b, dims):
    return lax.dot_general(a, b, (dims, ((), ())), preferred_element_type=F32)


MM = ((1,), (0,))
NT = ((1,), (1,))
TN = ((0,), (0,))


def one_hot(ids, count):
    return (ids[:, None] == lax.broadcasted_iota(I32, (1, count), 1)).astype(BF)


def widen(rows):
    half = rows.shape[-1] // 2
    pad = [(0, 0)] * (rows.ndim - 1) + [(0, HALF - half)]
    return jnp.concatenate([jnp.pad(rows[..., :half], pad), jnp.pad(rows[..., half:], pad)], -1)


def narrow(rows, width):
    half = width // 2
    return jnp.concatenate([rows[..., :half], rows[..., HALF : HALF + half]], -1)


def mask_of(shape, ids_row, base=0):
    return (lax.broadcasted_iota(I32, shape, 0) + base == ids_row).astype(BF)


def two_part_dot(mask, x, dims=MM):
    hi = x.astype(BF)
    lo = (x - hi.astype(F32)).astype(BF)
    return dot(mask, hi, dims) + dot(mask, lo, dims)


def power_of(x):
    peak = jnp.max(jnp.abs(x), keepdims=True)
    power = jnp.floor(jnp.log(jnp.maximum(peak, 1e-30)) * 1.4426950408889634)
    return jnp.clip(power, -90.0, 90.0)


def packed(x, power):
    lane = lax.broadcasted_iota(I32, x.shape, x.ndim - 1)
    return jnp.where(lane >= FULL - 8, power, x * jnp.exp2(12.0 - power))


def unpacked(x):
    lane = lax.broadcasted_iota(I32, x.shape, x.ndim - 1)
    scale = jnp.exp2(x[..., FULL - 1 :] - 12.0)
    return jnp.where(lane >= FULL - 8, 0.0, x * scale)


def with_rel(rel, v):
    v_re, v_im, r_re, r_im = v[:, :HALF], v[:, HALF:], rel[:, :HALF], rel[:, HALF:]
    return jnp.concatenate([v_re * r_re - v_im * r_im, v_re * r_im + v_im * r_re], axis=1)


def against_rel(rel, v):
    v_re, v_im, r_re, r_im = v[:, :HALF], v[:, HALF:], rel[:, :HALF], rel[:, HALF:]
    return jnp.concatenate([r_re * v_re + r_im * v_im, r_re * v_im - r_im * v_re], axis=1)


def edge_kernel(
    tail_col, slot_col, slot_row, tail_slot_row, rel_ref, rows_ref, hot_ref, tail_msg, back_msg, acc
):
    step = pl.program_id(0)
    edges = slot_col.shape[0]
    slots = rows_ref.shape[0]
    chunk = hot_ref.shape[0]

    @pl.when(step == 0)
    def _():
        acc[...] = jnp.zeros_like(acc)

    pick = tail_col[...] - step * chunk == lax.broadcasted_iota(I32, (edges, chunk), 1)
    acc[...] += dot(pick.astype(BF), hot_ref[...], MM)

    @pl.when(step == pl.num_programs(0) - 1)
    def _():
        rel = rel_ref[...]
        per = 24
        head_pick = (slot_col[...] == lax.broadcasted_iota(I32, (edges, slots), 1)).astype(BF)
        head_f = dot(head_pick, rows_ref[...], MM)
        n_neg = slots // per * (per - HEAD_CAP)
        j = lax.broadcasted_iota(I32, (n_neg, slots), 0)
        neg_slot = (j >> 3) * per + HEAD_CAP + (j & 7)
        neg_pick = (neg_slot == lax.broadcasted_iota(I32, (n_neg, slots), 1)).astype(BF)
        negatives = dot(neg_pick, rows_ref[...], MM).astype(BF)
        tail_f = acc[...]
        queries = with_rel(rel, head_f)
        probes = against_rel(rel, tail_f)
        positive = jnp.sum(queries * tail_f, axis=1, keepdims=True)
        query_b = queries.astype(BF)
        probe_b = probes.astype(BF)
        pos_weight = -jax.nn.sigmoid(-positive)
        tail_weight = jax.nn.sigmoid(dot(query_b, negatives, NT)).astype(BF)
        head_weight = jax.nn.sigmoid(dot(probe_b, negatives, NT)).astype(BF)
        tail_mix = dot(tail_weight, negatives, MM)
        head_mix = dot(head_weight, negatives, MM)
        head_grad = against_rel(rel, pos_weight * tail_f + tail_mix).astype(BF)
        tail_grad = with_rel(rel, pos_weight * head_f + head_mix)
        neg_grad = dot(tail_weight, query_b, TN) + dot(head_weight, probe_b, TN)

        tail_slots = tail_msg.shape[0]
        sums = two_part_dot(mask_of((tail_slots, edges), tail_slot_row[...]), tail_grad)
        tail_msg[...] = packed(sums, power_of(sums))
        back = dot(mask_of((slots, edges), slot_row[...]), head_grad, MM)
        back = back + two_part_dot(neg_pick, neg_grad, TN)
        back_msg[...] = packed(back, power_of(back))


def edge_call(tail_ids, head_slot, tail_slot, rel, rows, hot_all, tail_slots):
    edges = tail_ids.shape[0]
    slots = rows.shape[0]
    hot = hot_all.shape[0]
    steps = 8
    whole = lambda shape: pl.BlockSpec(shape, lambda i: (0, 0))
    return pl.pallas_call(
        edge_kernel,
        grid=(steps,),
        in_specs=[
            whole((edges, 1)),
            whole((edges, 1)),
            whole((1, edges)),
            whole((1, edges)),
            whole((edges, FULL)),
            whole((slots, FULL)),
            pl.BlockSpec((hot // steps, FULL), lambda i: (i, 0)),
        ],
        out_specs=[whole((tail_slots, FULL)), whole((slots, FULL))],
        out_shape=[
            jax.ShapeDtypeStruct((tail_slots, FULL), F32),
            jax.ShapeDtypeStruct((slots, FULL), F32),
        ],
        scratch_shapes=[pltpu.VMEM((edges, FULL), F32)],
        cost_estimate=pl.CostEstimate(flops=12 << 30, bytes_accessed=24 << 20, transcendentals=1 << 20),
        name="edge",
    )(
        tail_ids[:, None],
        head_slot[:, None],
        head_slot[None, :],
        tail_slot[None, :],
        rel,
        rows,
        hot_all,
    )


def rotated(src, own_ref, msg_ref, me, n_rep):
    own_ref[...] = src(me)
    for k in range(1, n_rep):
        part = src(lax.rem(me + k, n_rep))
        msg_ref[k - 1] = packed(part, power_of(part))


def dense_kernel(me_ref, ids_ref, got_ref, own_ref, msg_ref, dense, *, n_rep):
    near, slots, _ = got_ref.shape
    n_ring, rows, _ = dense.shape
    for z in range(n_ring):
        part = unpacked(got_ref[:, z * TAIL_CAP : (z + 1) * TAIL_CAP, :])
        part = part.reshape(near * TAIL_CAP, FULL)
        mask = mask_of((rows, near * TAIL_CAP), ids_ref[z : z + 1, :])
        dense[z] = two_part_dot(mask, part)
    quarter = rows // n_rep

    def src(q):
        start = pl.multiple_of(q * quarter, quarter)
        return dense[:, pl.ds(start, quarter), :].reshape(n_ring * quarter, FULL)

    rotated(src, own_ref, msg_ref, me_ref[0], n_rep)


def cold_kernel(me_ref, ids_ref, neg_ref, back_ref, own_ref, msg_ref, total, *, n_rep):
    n_src, per, _ = back_ref.shape
    rows = total.shape[0]
    back = unpacked(back_ref[...])
    negs = per - HEAD_CAP
    neg_sum = jnp.sum(back[:, HEAD_CAP:, :], axis=0)
    flat = back.reshape(n_src * per, FULL).astype(BF)
    mask = mask_of((rows, n_src * per), ids_ref[...])
    neg_mask = mask_of((rows, negs), neg_ref[...])
    hi = neg_sum.astype(BF)
    rest = neg_sum - hi.astype(F32)
    total[...] = dot(mask, flat, MM) + dot(neg_mask, hi, MM) + two_part_dot(neg_mask, rest)
    quarter = rows // n_rep

    def src(q):
        return total[pl.ds(pl.multiple_of(q * quarter, quarter), quarter), :]

    rotated(src, own_ref, msg_ref, me_ref[0], n_rep)


def smem():
    return pl.BlockSpec(memory_space=pltpu.SMEM)


def vmem():
    return pl.BlockSpec(memory_space=pltpu.VMEM)


def rotate_call(kernel, name, me, operands, rows, scratch, n_rep):
    return pl.pallas_call(
        functools.partial(kernel, n_rep=n_rep),
        in_specs=[smem()] + [vmem()] * len(operands),
        out_specs=[vmem(), vmem()],
        out_shape=[
            jax.ShapeDtypeStruct((rows, FULL), F32),
            jax.ShapeDtypeStruct((n_rep - 1, rows, FULL), F32),
        ],
        scratch_shapes=[pltpu.VMEM(scratch, F32)],
        cost_estimate=pl.CostEstimate(flops=4 << 30, bytes_accessed=8 << 20, transcendentals=0),
        name=name,
    )(me, *operands)


def shift(x, step, n_rep):
    return lax.ppermute(x, "rep", [(i, (i + step) % n_rep) for i in range(n_rep)])


def sum_kernel(own_ref, got_ref, msg_ref):
    total = own_ref[...]
    for k in range(got_ref.shape[0]):
        total = total + unpacked(got_ref[k])
    msg_ref[...] = packed(total, power_of(total))


def update_kernel(me_ref, table_ref, state_ref, msg_ref, table_out, state_out):
    width = table_ref.shape[1]
    grad = narrow(unpacked(msg_ref[0]), width)
    state = state_ref[...] + jnp.sum(grad * grad, axis=1, keepdims=True) / width
    state_out[...] = state
    table_out[...] = table_ref[...] - learn_rate * grad / jnp.sqrt(state)


def cold_update(me, table, state, msgs, n_rep):
    rows, width = table.shape
    quarter = rows // n_rep
    at = lambda k, me: (lax.rem(me[0] - k + n_rep, n_rep), 0)
    new_table, new_state = pl.pallas_call(
        update_kernel,
        grid_spec=pltpu.PrefetchScalarGridSpec(
            num_scalar_prefetch=1,
            grid=(n_rep,),
            in_specs=[
                pl.BlockSpec((quarter, width), at),
                pl.BlockSpec((quarter, 1), at),
                pl.BlockSpec((1, quarter, FULL), lambda k, me: (k, 0, 0)),
            ],
            out_specs=[pl.BlockSpec((quarter, width), at), pl.BlockSpec((quarter, 1), at)],
        ),
        out_shape=[
            jax.ShapeDtypeStruct((rows, width), F32),
            jax.ShapeDtypeStruct((rows, 1), F32),
        ],
        name="update",
    )(me, table, state[:, None], msgs)
    return new_table, new_state[:, 0]


def adagrad(weights, state, grad):
    new_state = state + jnp.mean(grad * grad, axis=1)
    return (weights - learn_rate * grad / jnp.sqrt(new_state)[:, None], new_state)


def per_device(
    cold_table,
    cold_state,
    hot_table,
    hot_state,
    relations,
    head_owner,
    head_row,
    edge_rel,
    edge_tail,
    neg_ids,
):
    n_table = lax.axis_size("table")
    n_rep = lax.axis_size("rep")
    n_ring = n_table // GROUP
    edges = head_row.shape[0]
    width = cold_table.shape[1]
    cold_rows = cold_table.shape[0]
    hot_rows = hot_table.shape[0]
    negs = neg_ids.shape[1]
    near = [[z * GROUP + g for g in range(GROUP)] for z in range(n_ring)]
    far = [[z * GROUP + g for z in range(n_ring)] for g in range(GROUP)]

    per = HEAD_CAP + negs
    me = lax.axis_index("rep").astype(I32).reshape(1)

    hot_all = lax.all_gather(widen(hot_table.astype(BF)), "table", axis=0, tiled=True)
    cold_bf = widen(cold_table.astype(BF))

    owner_hot = one_hot(head_owner[:, 0], n_table)
    row = lax.broadcasted_iota(jnp.int32, (edges, edges), 0)
    col = lax.broadcasted_iota(jnp.int32, (edges, edges), 1)
    before = dot((col < row).astype(BF), owner_hot, ((1,), (0,)))
    rank = jnp.sum(before * owner_hot.astype(F32), axis=1).astype(jnp.int32)
    head_slot = head_owner[:, 0] * per + rank

    block = edge_tail // hot_rows
    within = edge_tail % hot_rows
    block_hot = one_hot(block, n_table)
    within_hot = one_hot(within, hot_rows)
    present = (dot(block_hot, within_hot, ((0,), (0,))) > 0.5).astype(BF)
    prow = lax.broadcasted_iota(jnp.int32, (hot_rows, hot_rows), 0)
    pcol = lax.broadcasted_iota(jnp.int32, (hot_rows, hot_rows), 1)
    ranks = dot(present, (prow < pcol).astype(BF), ((1,), (0,)))
    rank_of = dot(block_hot, ranks.astype(BF), ((1,), (0,)))
    tail_rank = jnp.sum(rank_of * within_hot.astype(F32), axis=1).astype(jnp.int32)
    z_of, g_of = block // GROUP, block % GROUP
    tail_slot = (g_of * n_ring + z_of) * TAIL_CAP + tail_rank
    slot_iota = lax.broadcasted_iota(jnp.int32, (n_table, hot_rows, TAIL_CAP), 2)
    match = (ranks.astype(jnp.int32)[:, :, None] == slot_iota) & (present > 0.5)[:, :, None]
    row_iota = lax.broadcasted_iota(jnp.int32, (n_table, hot_rows, TAIL_CAP), 1) + 1
    slot_rows = jnp.sum(jnp.where(match, row_iota, 0), axis=1) - 1
    slot_rows = slot_rows.reshape(n_ring, GROUP, TAIL_CAP).transpose(1, 0, 2)

    wanted = jnp.zeros((n_table * per,), I32).at[head_slot].set(head_row).reshape(n_table, per)
    wanted = lax.all_to_all(wanted[:, :HEAD_CAP], "table", 0, 0)
    dense_rows = lax.all_to_all(
        slot_rows.reshape(GROUP, n_ring * TAIL_CAP), "table", 0, 0, axis_index_groups=near
    )
    dense_ids = dense_rows.reshape(GROUP, n_ring, TAIL_CAP).transpose(1, 0, 2)
    dense_ids = dense_ids.reshape(n_ring, GROUP * TAIL_CAP)
    own_negs = jnp.broadcast_to(neg_ids[0][None, :], (n_table, negs))
    asked = jnp.concatenate([wanted, own_negs], axis=1)
    head_ids = jnp.concatenate([wanted, jnp.full((n_table, negs), -1, I32)], axis=1)
    rows = lax.all_to_all(cold_bf[asked], "table", 0, 0)
    relation = widen(relations[edge_rel])
    tail_msg, back_msg = edge_call(
        edge_tail,
        head_slot,
        tail_slot,
        relation,
        rows.reshape(n_table * per, FULL),
        hot_all,
        n_table * TAIL_CAP,
    )

    tail_got = lax.all_to_all(
        tail_msg.astype(F16).reshape(GROUP, n_ring * TAIL_CAP, FULL),
        "table",
        0,
        0,
        axis_index_groups=near,
    )
    back_msg, tail_got = lax.optimization_barrier((back_msg.astype(F16), tail_got))
    back = lax.all_to_all(back_msg.reshape(n_table, per, FULL), "table", 0, 0)

    quarter = hot_rows // n_rep
    hot_own, hot_msg = rotate_call(
        dense_kernel,
        "dense",
        me,
        (dense_ids, tail_got.astype(F32)),
        n_ring * quarter,
        (n_ring, hot_rows, FULL),
        n_rep,
    )
    hot_msg = hot_msg.astype(F16)
    hot_part = hot_own
    for k in range(1, n_rep):
        hot_part = hot_part + unpacked(shift(hot_msg[k - 1], k, n_rep).astype(F32))
    hot_part, back = lax.optimization_barrier((hot_part, back))
    hot_got = lax.all_to_all(
        hot_part.reshape(n_ring, quarter, FULL), "table", 0, 0, axis_index_groups=far
    )
    hot_sum = jnp.sum(hot_got, axis=0)

    cold_own, cold_msg = rotate_call(
        cold_kernel,
        "cold",
        me,
        (head_ids.reshape(1, n_table * per), neg_ids, back.astype(F32)),
        cold_rows // n_rep,
        (cold_rows, FULL),
        n_rep,
    )
    cold_msg = cold_msg.astype(F16)
    cold_got = jnp.stack([shift(cold_msg[k - 1], k, n_rep) for k in range(1, n_rep)])
    cold_part = pl.pallas_call(
        sum_kernel,
        in_specs=[vmem()] * 2,
        out_specs=vmem(),
        out_shape=jax.ShapeDtypeStruct((cold_rows // n_rep, FULL), F32),
        name="sum",
    )(cold_own, cold_got.astype(F32)).astype(F16)
    parts = jnp.stack([cold_part] + [shift(cold_part, k, n_rep) for k in range(1, n_rep)])
    new_cold_table, new_cold_state = cold_update(
        me, cold_table, cold_state, parts.astype(F32), n_rep
    )

    hot_parts = [hot_sum] + [shift(hot_sum, k, n_rep) for k in range(1, n_rep)]
    hot_total = jnp.zeros((n_rep, quarter, FULL), F32)
    for k, part in enumerate(hot_parts):
        hot_total = lax.dynamic_update_index_in_dim(
            hot_total, part, lax.rem(me[0] - k + n_rep, n_rep), 0
        )
    hot_total = narrow(hot_total.reshape(hot_rows, FULL), width)
    new_hot_table, new_hot_state = adagrad(hot_table, hot_state, hot_total)
    return (new_cold_table, new_cold_state, new_hot_table, new_hot_state)


def solution(mesh):
    in_specs = (
        P("table", None),
        P("table"),
        P("table", None),
        P("table"),
        P(),
        P(("rep", "table"), None),
        P(("rep", "table")),
        P(("rep", "table")),
        P(("rep", "table")),
        P("rep", "table"),
    )
    out_specs = (P("table", None), P("table"), P("table", None), P("table"))
    return jax.shard_map(
        per_device, mesh=mesh, in_specs=in_specs, out_specs=out_specs, check_vma=False
    )
```

```python
import functools
import jax
import jax.numpy as jnp
from jax import lax
from jax.experimental import pallas as pl
from jax.experimental.pallas import tpu as pltpu
from jax.sharding import PartitionSpec as P


learn_rate = 0.5
HEAD_CAP = 16
TAIL_CAP = 32
GROUP = 8
HALF = 256
FULL = 2 * HALF

BF = jnp.bfloat16
F16 = jnp.float16
F32 = jnp.float32
I32 = jnp.int32


def dot(a, b, dims):
    return lax.dot_general(a, b, (dims, ((), ())), preferred_element_type=F32)


MM = ((1,), (0,))
NT = ((1,), (1,))
TN = ((0,), (0,))


def one_hot(ids, count):
    return (ids[:, None] == lax.broadcasted_iota(I32, (1, count), 1)).astype(BF)


def widen(rows):
    half = rows.shape[-1] // 2
    pad = [(0, 0)] * (rows.ndim - 1) + [(0, HALF - half)]
    return jnp.concatenate([jnp.pad(rows[..., :half], pad), jnp.pad(rows[..., half:], pad)], -1)


def narrow(rows, width):
    half = width // 2
    return jnp.concatenate([rows[..., :half], rows[..., HALF : HALF + half]], -1)


def mask_of(shape, ids_row, base=0):
    return (lax.broadcasted_iota(I32, shape, 0) + base == ids_row).astype(BF)


def two_part_dot(mask, x, dims=MM):
    hi = x.astype(BF)
    lo = (x - hi.astype(F32)).astype(BF)
    return dot(mask, hi, dims) + dot(mask, lo, dims)


def power_of(x):
    peak = jnp.max(jnp.abs(x), keepdims=True)
    power = jnp.floor(jnp.log(jnp.maximum(peak, 1e-30)) * 1.4426950408889634)
    return jnp.clip(power, -90.0, 90.0)


def packed(x, power):
    lane = lax.broadcasted_iota(I32, x.shape, x.ndim - 1)
    return jnp.where(lane >= FULL - 8, power, x * jnp.exp2(12.0 - power))


def unpacked(x):
    lane = lax.broadcasted_iota(I32, x.shape, x.ndim - 1)
    scale = jnp.exp2(x[..., FULL - 1 :] - 12.0)
    return jnp.where(lane >= FULL - 8, 0.0, x * scale)


def with_rel(rel, v):
    v_re, v_im, r_re, r_im = v[:, :HALF], v[:, HALF:], rel[:, :HALF], rel[:, HALF:]
    return jnp.concatenate([v_re * r_re - v_im * r_im, v_re * r_im + v_im * r_re], axis=1)


def against_rel(rel, v):
    v_re, v_im, r_re, r_im = v[:, :HALF], v[:, HALF:], rel[:, :HALF], rel[:, HALF:]
    return jnp.concatenate([r_re * v_re + r_im * v_im, r_re * v_im - r_im * v_re], axis=1)


def edge_kernel(slot_col, slot_row, tail_col, tail_row, rel_ref, rows_ref, *refs):
    pieces, tail_msg, back_msg = refs[:GROUP], refs[GROUP], refs[GROUP + 1]
    found, negs, hi_buf, lo_buf, head_buf, neg_buf = refs[GROUP + 2 :]
    edges = slot_col.shape[0]
    slots = rows_ref.shape[0]
    part = pieces[0].shape[0]
    per = slots // (GROUP * GROUP)
    n_neg = negs.shape[0]
    for k in range(GROUP):
        found[k * part : (k + 1) * part, :] = pieces[k][...]
    halves = 2
    e_half, s_half, n_half = edges // halves, slots // halves, n_neg // halves
    j = lax.broadcasted_iota(I32, (n_half, 1), 0)
    neg_col = (j >> 3) * per + HEAD_CAP + (j & 7)
    j = lax.broadcasted_iota(I32, (1, n_half), 1)
    neg_row = (j >> 3) * per + HEAD_CAP + (j & 7)

    @pl.loop(0, halves)
    def _(c):
        at = pl.ds(pl.multiple_of(c * s_half, s_half), s_half)
        pick = (neg_col == lax.broadcasted_iota(I32, (n_half, s_half), 1)).astype(BF)
        to = pl.ds(pl.multiple_of(c * n_half, n_half), n_half)
        negs[to, :] = dot(pick, rows_ref[at, :], MM).astype(BF)

    neg_buf[...] = jnp.zeros_like(neg_buf)

    @pl.loop(0, halves)
    def _(h):
        at = pl.ds(pl.multiple_of(h * e_half, e_half), e_half)
        rel = rel_ref[at, :]
        pick = tail_col[at, :] == lax.broadcasted_iota(I32, (e_half, GROUP * part), 1)
        tail_f = dot(pick.astype(BF), found[...], MM)
        pick = slot_col[at, :] == lax.broadcasted_iota(I32, (e_half, slots), 1)
        head_f = dot(pick.astype(BF), rows_ref[...], MM)
        negatives = negs[...]
        queries = with_rel(rel, head_f)
        probes = against_rel(rel, tail_f)
        positive = jnp.sum(queries * tail_f, axis=1, keepdims=True)
        query_b = queries.astype(BF)
        probe_b = probes.astype(BF)
        pos_weight = -jax.nn.sigmoid(-positive)
        tail_weight = jax.nn.sigmoid(dot(query_b, negatives, NT)).astype(BF)
        head_weight = jax.nn.sigmoid(dot(probe_b, negatives, NT)).astype(BF)
        tail_mix = dot(tail_weight, negatives, MM)
        head_mix = dot(head_weight, negatives, MM)
        head_buf[at, :] = against_rel(rel, pos_weight * tail_f + tail_mix).astype(BF)
        tail_grad = with_rel(rel, pos_weight * head_f + head_mix)
        grad_hi = tail_grad.astype(BF)
        hi_buf[at, :] = grad_hi
        lo_buf[at, :] = (tail_grad - grad_hi.astype(F32)).astype(BF)
        neg_buf[...] += dot(tail_weight, query_b, TN) + dot(head_weight, probe_b, TN)

    @pl.loop(0, GROUP)
    def _(k):
        mask = mask_of((part, edges), tail_row[...], k * part)
        sums = dot(mask, hi_buf[...], MM) + dot(mask, lo_buf[...], MM)
        to = pl.ds(pl.multiple_of(k * part, part), part)
        tail_msg[to, :] = packed(sums, power_of(sums))

    def back_half(c, power):
        to = pl.ds(pl.multiple_of(c * s_half, s_half), s_half)
        back = dot(mask_of((s_half, edges), slot_row[...], c * s_half), head_buf[...], MM)
        grads = neg_buf[pl.ds(pl.multiple_of(c * n_half, n_half), n_half), :]
        back = back + two_part_dot(mask_of((s_half, n_half), neg_row), grads)
        back_msg[to, :] = back
        return jnp.maximum(power, power_of(back))

    power = lax.fori_loop(0, halves, back_half, jnp.full((1, 1), -90.0, F32))
    back_msg[...] = packed(back_msg[...], power)


def edge_call(head_slot, tail_slot, rel, rows, pieces):
    edges = head_slot.shape[0]
    slots = rows.shape[0]
    part = pieces[0].shape[0]
    n_neg = slots - GROUP * GROUP * HEAD_CAP
    return pl.pallas_call(
        edge_kernel,
        in_specs=[vmem()] * (6 + GROUP),
        out_specs=[vmem()] * 2,
        out_shape=[
            jax.ShapeDtypeStruct((GROUP * part, FULL), F32),
            jax.ShapeDtypeStruct((slots, FULL), F32),
        ],
        scratch_shapes=[
            pltpu.VMEM((GROUP * part, FULL), BF),
            pltpu.VMEM((n_neg, FULL), BF),
            pltpu.VMEM((edges, FULL), BF),
            pltpu.VMEM((edges, FULL), BF),
            pltpu.VMEM((edges, FULL), BF),
            pltpu.VMEM((n_neg, FULL), F32),
        ],
        cost_estimate=pl.CostEstimate(flops=9 << 30, bytes_accessed=16 << 20, transcendentals=1 << 20),
        name="edge",
    )(
        head_slot[:, None],
        head_slot[None, :],
        tail_slot[:, None],
        tail_slot[None, :],
        rel,
        rows,
        *pieces,
    )


def answer_kernel(me_ref, ids_ref, *refs):
    n_ring = len(refs) - GROUP
    blocks, outs = refs[:n_ring], refs[n_ring:]
    rows = blocks[0].shape[0]
    for k in range(n_ring):
        z = lax.rem(me_ref[0] - k + n_ring, n_ring)
        mask = mask_of((rows, GROUP * TAIL_CAP), ids_ref[pl.ds(z, 1), :])
        found = dot(mask, blocks[k][...], TN).astype(BF)
        for g in range(GROUP):
            start = pl.multiple_of(z * TAIL_CAP, TAIL_CAP)
            outs[g][pl.ds(start, TAIL_CAP), :] = found[g * TAIL_CAP : (g + 1) * TAIL_CAP, :]


def answer_call(ring_me, ids, blocks):
    n_ring = len(blocks)
    return pl.pallas_call(
        answer_kernel,
        in_specs=[smem()] + [vmem()] * (1 + n_ring),
        out_specs=[vmem()] * GROUP,
        out_shape=[jax.ShapeDtypeStruct((n_ring * TAIL_CAP, FULL), BF)] * GROUP,
        cost_estimate=pl.CostEstimate(flops=1 << 30, bytes_accessed=4 << 20, transcendentals=0),
        name="answer",
    )(ring_me, ids, *blocks)


def scaled_parts(src, out_ref, me, n_rep):
    @pl.loop(0, n_rep)
    def _(k):
        part = src(lax.rem(me + k, n_rep))
        out_ref[k] = jnp.where(k == 0, part, packed(part, power_of(part)))


def dense_kernel(me_ref, ids_ref, *refs, n_rep):
    got, out_ref, dense = refs[:GROUP], refs[GROUP], refs[GROUP + 1]
    n_ring, rows, _ = dense.shape

    @pl.loop(0, n_ring)
    def _(z):
        at = pl.ds(pl.multiple_of(z * TAIL_CAP, TAIL_CAP), TAIL_CAP)
        part = [unpacked(got[g][at, :]) for g in range(GROUP)]
        mask = mask_of((rows, GROUP * TAIL_CAP), ids_ref[pl.ds(z, 1), :])
        dense[z] = two_part_dot(mask, jnp.concatenate(part, axis=0))

    quarter = rows // n_rep

    def src(q):
        start = pl.multiple_of(q * quarter, quarter)
        return dense[:, pl.ds(start, quarter), :].reshape(n_ring * quarter, FULL)

    scaled_parts(src, out_ref, me_ref[0], n_rep)


def cold_kernel(me_ref, ids_ref, neg_ref, back_ref, out_ref, flat, *, n_rep):
    n_src, per, _ = back_ref.shape
    quarter = out_ref.shape[1]
    back = unpacked(back_ref[...])
    negs = per - HEAD_CAP
    neg_sum = jnp.sum(back[:, HEAD_CAP:, :], axis=0)
    flat[...] = back.reshape(n_src * per, FULL).astype(BF)
    hi = neg_sum.astype(BF)
    rest = neg_sum - hi.astype(F32)

    def src(q):
        mask = mask_of((quarter, n_src * per), ids_ref[...], q * quarter)
        neg_mask = mask_of((quarter, negs), neg_ref[...], q * quarter)
        return dot(mask, flat[...], MM) + dot(neg_mask, hi, MM) + two_part_dot(neg_mask, rest)

    scaled_parts(src, out_ref, me_ref[0], n_rep)


def smem():
    return pl.BlockSpec(memory_space=pltpu.SMEM)


def vmem():
    return pl.BlockSpec(memory_space=pltpu.VMEM)


def parts_call(kernel, me, operands, rows, scratch, n_rep):
    return pl.pallas_call(
        functools.partial(kernel, n_rep=n_rep),
        in_specs=[smem()] + [vmem()] * len(operands),
        out_specs=vmem(),
        out_shape=jax.ShapeDtypeStruct((n_rep, rows, FULL), F32),
        scratch_shapes=[scratch],
        cost_estimate=pl.CostEstimate(flops=4 << 30, bytes_accessed=8 << 20, transcendentals=0),
    )(me, *operands)


def shift(x, step, n_rep):
    return lax.ppermute(x, "rep", [(i, (i + step) % n_rep) for i in range(n_rep)])


def ring_shift(x, step, n_table):
    return lax.ppermute(x, "table", [(i, (i + step * GROUP) % n_table) for i in range(n_table)])


def near_swap(x, other, n_table):
    return lax.ppermute(x, "table", [(i, i ^ other) for i in range(n_table)])


def sum_kernel(own_ref, got_ref, msg_ref):
    total = own_ref[0]
    for k in range(got_ref.shape[0]):
        total = total + unpacked(got_ref[k])
    msg_ref[...] = packed(total, power_of(total))


def update_kernel(me_ref, table_ref, state_ref, msg_ref, table_out, state_out):
    width = table_ref.shape[1]
    grad = narrow(unpacked(msg_ref[0]), width)
    state = state_ref[...] + jnp.sum(grad * grad, axis=1, keepdims=True) / width
    state_out[...] = state
    table_out[...] = table_ref[...] - learn_rate * grad / jnp.sqrt(state)


def cold_update(me, table, state, msgs, n_rep):
    rows, width = table.shape
    quarter = rows // n_rep
    at = lambda k, me: (lax.rem(me[0] - k + n_rep, n_rep), 0)
    new_table, new_state = pl.pallas_call(
        update_kernel,
        grid_spec=pltpu.PrefetchScalarGridSpec(
            num_scalar_prefetch=1,
            grid=(n_rep,),
            in_specs=[
                pl.BlockSpec((quarter, width), at),
                pl.BlockSpec((quarter, 1), at),
                pl.BlockSpec((1, quarter, FULL), lambda k, me: (k, 0, 0)),
            ],
            out_specs=[pl.BlockSpec((quarter, width), at), pl.BlockSpec((quarter, 1), at)],
        ),
        out_shape=[
            jax.ShapeDtypeStruct((rows, width), F32),
            jax.ShapeDtypeStruct((rows, 1), F32),
        ],
        name="update",
    )(me, table, state[:, None], msgs)
    return new_table, new_state[:, 0]


def adagrad(weights, state, grad):
    new_state = state + jnp.mean(grad * grad, axis=1)
    return (weights - learn_rate * grad / jnp.sqrt(new_state)[:, None], new_state)


def per_device(
    cold_table,
    cold_state,
    hot_table,
    hot_state,
    relations,
    head_owner,
    head_row,
    edge_rel,
    edge_tail,
    neg_ids,
):
    n_table = lax.axis_size("table")
    n_rep = lax.axis_size("rep")
    n_ring = n_table // GROUP
    edges = head_row.shape[0]
    width = cold_table.shape[1]
    cold_rows = cold_table.shape[0]
    hot_rows = hot_table.shape[0]
    negs = neg_ids.shape[1]
    near = [[z * GROUP + g for g in range(GROUP)] for z in range(n_ring)]
    far = [[z * GROUP + g for z in range(n_ring)] for g in range(GROUP)]

    per = HEAD_CAP + negs
    me = lax.axis_index("rep").astype(I32).reshape(1)

    place = lax.axis_index("table").astype(I32)
    ring_me, near_me = (place // GROUP).reshape(1), place % GROUP

    hot_bf = widen(hot_table.astype(BF))
    blocks = [hot_bf]
    for k in range(1, n_ring):
        blocks.append(ring_shift(hot_bf, k, n_table))
    cold_bf = widen(cold_table.astype(BF))

    owner_hot = one_hot(head_owner[:, 0], n_table)
    row = lax.broadcasted_iota(jnp.int32, (edges, edges), 0)
    col = lax.broadcasted_iota(jnp.int32, (edges, edges), 1)
    before = dot((col < row).astype(BF), owner_hot, ((1,), (0,)))
    rank = jnp.sum(before * owner_hot.astype(F32), axis=1).astype(jnp.int32)
    head_slot = head_owner[:, 0] * per + rank

    block = edge_tail // hot_rows
    within = edge_tail % hot_rows
    block_hot = one_hot(block, n_table)
    within_hot = one_hot(within, hot_rows)
    present = (dot(block_hot, within_hot, ((0,), (0,))) > 0.5).astype(BF)
    prow = lax.broadcasted_iota(jnp.int32, (hot_rows, hot_rows), 0)
    pcol = lax.broadcasted_iota(jnp.int32, (hot_rows, hot_rows), 1)
    ranks = dot(present, (prow < pcol).astype(BF), ((1,), (0,)))
    rank_of = dot(block_hot, ranks.astype(BF), ((1,), (0,)))
    tail_rank = jnp.sum(rank_of * within_hot.astype(F32), axis=1).astype(jnp.int32)
    z_of, g_of = block // GROUP, block % GROUP
    tail_slot = ((g_of ^ near_me) * n_ring + z_of) * TAIL_CAP + tail_rank
    slot_iota = lax.broadcasted_iota(jnp.int32, (n_table, hot_rows, TAIL_CAP), 2)
    match = (ranks.astype(jnp.int32)[:, :, None] == slot_iota) & (present > 0.5)[:, :, None]
    row_iota = lax.broadcasted_iota(jnp.int32, (n_table, hot_rows, TAIL_CAP), 1) + 1
    slot_rows = jnp.sum(jnp.where(match, row_iota, 0), axis=1) - 1
    slot_rows = slot_rows.reshape(n_ring, GROUP, TAIL_CAP).transpose(1, 0, 2)

    wanted = jnp.zeros((n_table * per,), I32).at[head_slot].set(head_row).reshape(n_table, per)
    wanted = lax.all_to_all(wanted[:, :HEAD_CAP], "table", 0, 0)
    dense_rows = lax.all_to_all(
        slot_rows.reshape(GROUP, n_ring * TAIL_CAP), "table", 0, 0, axis_index_groups=near
    )
    dense_ids = dense_rows.reshape(GROUP, n_ring, TAIL_CAP)[jnp.arange(GROUP) ^ near_me]
    dense_ids = dense_ids.transpose(1, 0, 2).reshape(n_ring, GROUP * TAIL_CAP)
    own_negs = jnp.broadcast_to(neg_ids[0][None, :], (n_table, negs))
    asked = jnp.concatenate([wanted, own_negs], axis=1)
    head_ids = jnp.concatenate([wanted, jnp.full((n_table, negs), -1, I32)], axis=1)
    rows = lax.all_to_all(cold_bf[asked], "table", 0, 0)
    relation = widen(relations[edge_rel])
    found = answer_call(ring_me, dense_ids, blocks)
    pieces = [found[0]] + [near_swap(found[g], g, n_table) for g in range(1, GROUP)]
    tail_msg, back_msg = edge_call(
        head_slot, tail_slot, relation, rows.reshape(n_table * per, FULL), pieces
    )

    tail_msgs = tail_msg.reshape(GROUP, n_ring * TAIL_CAP, FULL)
    tail_msgs = [tail_msgs[g].astype(F16) for g in range(GROUP)]
    tail_got = [tail_msgs[0]] + [near_swap(tail_msgs[g], g, n_table) for g in range(1, GROUP)]
    back = lax.all_to_all(back_msg.astype(F16).reshape(n_table, per, FULL), "table", 0, 0)

    quarter = hot_rows // n_rep
    hot_parts = parts_call(
        dense_kernel,
        me,
        (dense_ids, *[got.astype(F32) for got in tail_got]),
        n_ring * quarter,
        pltpu.VMEM((n_ring, hot_rows, FULL), F32),
        n_rep,
    )
    hot_msg = hot_parts[1:].astype(F16)
    hot_part = hot_parts[0]
    for k in range(1, n_rep):
        hot_part = hot_part + unpacked(shift(hot_msg[k - 1], k, n_rep).astype(F32))
    hot_part, back = lax.optimization_barrier((hot_part, back))
    hot_got = lax.all_to_all(
        hot_part.reshape(n_ring, quarter, FULL), "table", 0, 0, axis_index_groups=far
    )
    hot_sum = jnp.sum(hot_got, axis=0)

    cold_parts = parts_call(
        cold_kernel,
        me,
        (head_ids.reshape(1, n_table * per), neg_ids, back.astype(F32)),
        cold_rows // n_rep,
        pltpu.VMEM((n_table * per, FULL), BF),
        n_rep,
    )
    cold_msg = cold_parts[1:].astype(F16)
    cold_got = jnp.stack([shift(cold_msg[k - 1], k, n_rep) for k in range(1, n_rep)])
    cold_part = pl.pallas_call(
        sum_kernel,
        in_specs=[pl.BlockSpec((1, cold_rows // n_rep, FULL), lambda i: (0, 0, 0)), pl.BlockSpec((n_rep - 1, cold_rows // n_rep, FULL), lambda i: (0, 0, 0))],
        grid=(1,),
        out_specs=pl.BlockSpec((cold_rows // n_rep, FULL), lambda i: (0, 0)),
        out_shape=jax.ShapeDtypeStruct((cold_rows // n_rep, FULL), F32),
        name="sum",
    )(cold_parts, cold_got.astype(F32)).astype(F16)
    cold_part, hot_sum = lax.optimization_barrier((cold_part, hot_sum))
    parts = jnp.stack([cold_part] + [shift(cold_part, k, n_rep) for k in range(1, n_rep)])
    new_cold_table, new_cold_state = cold_update(
        me, cold_table, cold_state, parts.astype(F32), n_rep
    )

    hot_parts = [hot_sum] + [shift(hot_sum, k, n_rep) for k in range(1, n_rep)]
    hot_total = jnp.zeros((n_rep, quarter, FULL), F32)
    for k, part in enumerate(hot_parts):
        hot_total = lax.dynamic_update_index_in_dim(
            hot_total, part, lax.rem(me[0] - k + n_rep, n_rep), 0
        )
    hot_total = narrow(hot_total.reshape(hot_rows, FULL), width)
    new_hot_table, new_hot_state = adagrad(hot_table, hot_state, hot_total)
    return (new_cold_table, new_cold_state, new_hot_table, new_hot_state)


def solution(mesh):
    in_specs = (
        P("table", None),
        P("table"),
        P("table", None),
        P("table"),
        P(),
        P(("rep", "table"), None),
        P(("rep", "table")),
        P(("rep", "table")),
        P(("rep", "table")),
        P("rep", "table"),
    )
    out_specs = (P("table", None), P("table"), P("table", None), P("table"))

    return jax.shard_map(
        per_device, mesh=mesh, in_specs=in_specs, out_specs=out_specs, check_vma=False
    )
```

```python
import functools
import jax
import jax.numpy as jnp
from jax import lax
from jax.experimental import pallas as pl
from jax.experimental.pallas import tpu as pltpu
from jax.sharding import PartitionSpec as P


learn_rate = 0.5
HEAD_CAP = 16
TAIL_CAP = 32
GROUP = 8
HALF = 256
FULL = 2 * HALF

BF = jnp.bfloat16
I16 = jnp.int16
F32 = jnp.float32
I32 = jnp.int32


def dot(a, b, dims):
    return lax.dot_general(a, b, (dims, ((), ())), preferred_element_type=F32)


MM = ((1,), (0,))
NT = ((1,), (1,))
TN = ((0,), (0,))


def one_hot(ids, count):
    return (ids[:, None] == lax.broadcasted_iota(I32, (1, count), 1)).astype(BF)


def widen(rows):
    half = rows.shape[-1] // 2
    pad = [(0, 0)] * (rows.ndim - 1) + [(0, HALF - half)]
    return jnp.concatenate([jnp.pad(rows[..., :half], pad), jnp.pad(rows[..., half:], pad)], -1)


def narrow(rows, width):
    half = width // 2
    return jnp.concatenate([rows[..., :half], rows[..., HALF : HALF + half]], -1)


def mask_of(shape, ids_row, base=0):
    return (lax.broadcasted_iota(I32, shape, 0) + base == ids_row).astype(BF)


def two_part_dot(mask, x, dims=MM):
    hi = x.astype(BF)
    lo = (x - hi.astype(F32)).astype(BF)
    return dot(mask, hi, dims) + dot(mask, lo, dims)


def packed(x):
    peak = jnp.max(jnp.abs(x), axis=-1, keepdims=True)
    power = jnp.floor(jnp.log(jnp.maximum(peak, 1e-30)) * 1.4426950408889634)
    code = jnp.round(x * jnp.exp2(14.0 - power))
    lane = lax.broadcasted_iota(I32, x.shape, x.ndim - 1)
    code = jnp.where(lane >= FULL - 8, power, jnp.clip(code, -32767.0, 32767.0))
    return code.astype(I32).astype(I16)


def unpacked(code):
    x = code.astype(F32)
    lane = lax.broadcasted_iota(I32, x.shape, x.ndim - 1)
    scale = jnp.exp2(x[..., FULL - 1 :] - 14.0)
    return jnp.where(lane >= FULL - 8, 0.0, x * scale)


def with_rel(rel, v):
    v_re, v_im, r_re, r_im = v[:, :HALF], v[:, HALF:], rel[:, :HALF], rel[:, HALF:]
    return jnp.concatenate([v_re * r_re - v_im * r_im, v_re * r_im + v_im * r_re], axis=1)


def against_rel(rel, v):
    v_re, v_im, r_re, r_im = v[:, :HALF], v[:, HALF:], rel[:, :HALF], rel[:, HALF:]
    return jnp.concatenate([r_re * v_re + r_im * v_im, r_re * v_im - r_im * v_re], axis=1)


def put(ref, value):
    ref[...] = value


def edge_kernel(slot_col, slot_row, tail_col, tail_row, rel_ref, rows_ref, *refs):
    pieces, tail_msgs, back_msg = refs[:GROUP], refs[GROUP : 2 * GROUP], refs[2 * GROUP]
    found, negs, hi_buf, lo_buf, head_buf, neg_buf = refs[2 * GROUP + 1 :]
    edges = slot_col.shape[0]
    slots = rows_ref.shape[0]
    part = pieces[0].shape[0]
    per = slots // (GROUP * GROUP)
    n_neg = negs.shape[0]
    for k in range(GROUP):
        found[k * part : (k + 1) * part, :] = pieces[k][...]
    halves = 2
    e_half, s_half, n_half = edges // halves, slots // halves, n_neg // halves
    j = lax.broadcasted_iota(I32, (n_half, 1), 0)
    neg_col = (j >> 3) * per + HEAD_CAP + (j & 7)
    j = lax.broadcasted_iota(I32, (1, n_half), 1)
    neg_row = (j >> 3) * per + HEAD_CAP + (j & 7)

    @pl.loop(0, halves)
    def _(c):
        at = pl.ds(pl.multiple_of(c * s_half, s_half), s_half)
        pick = (neg_col == lax.broadcasted_iota(I32, (n_half, s_half), 1)).astype(BF)
        to = pl.ds(pl.multiple_of(c * n_half, n_half), n_half)
        negs[to, :] = dot(pick, rows_ref[at, :], MM).astype(BF)

    neg_buf[...] = jnp.zeros_like(neg_buf)

    @pl.loop(0, halves)
    def _(h):
        at = pl.ds(pl.multiple_of(h * e_half, e_half), e_half)
        rel = rel_ref[at, :]
        pick = tail_col[at, :] == lax.broadcasted_iota(I32, (e_half, GROUP * part), 1)
        tail_f = dot(pick.astype(BF), found[...], MM)
        pick = slot_col[at, :] == lax.broadcasted_iota(I32, (e_half, slots), 1)
        head_f = dot(pick.astype(BF), rows_ref[...], MM)
        negatives = negs[...]
        queries = with_rel(rel, head_f)
        probes = against_rel(rel, tail_f)
        positive = jnp.sum(queries * tail_f, axis=1, keepdims=True)
        query_b = queries.astype(BF)
        probe_b = probes.astype(BF)
        pos_weight = -jax.nn.sigmoid(-positive)
        tail_weight = jax.nn.sigmoid(dot(query_b, negatives, NT)).astype(BF)
        head_weight = jax.nn.sigmoid(dot(probe_b, negatives, NT)).astype(BF)
        tail_mix = dot(tail_weight, negatives, MM)
        head_mix = dot(head_weight, negatives, MM)
        head_buf[at, :] = against_rel(rel, pos_weight * tail_f + tail_mix).astype(BF)
        tail_grad = with_rel(rel, pos_weight * head_f + head_mix)
        grad_hi = tail_grad.astype(BF)
        hi_buf[at, :] = grad_hi
        lo_buf[at, :] = (tail_grad - grad_hi.astype(F32)).astype(BF)
        neg_buf[...] += dot(tail_weight, query_b, TN) + dot(head_weight, probe_b, TN)

    @pl.loop(0, GROUP)
    def _(k):
        mask = mask_of((part, edges), tail_row[...], k * part)
        code = packed(dot(mask, hi_buf[...], MM) + dot(mask, lo_buf[...], MM))
        for g in range(GROUP):
            pl.when(k == g)(functools.partial(put, tail_msgs[g], code))

    @pl.loop(0, halves)
    def _(c):
        to = pl.ds(pl.multiple_of(c * s_half, s_half), s_half)
        back = dot(mask_of((s_half, edges), slot_row[...], c * s_half), head_buf[...], MM)
        grads = neg_buf[pl.ds(pl.multiple_of(c * n_half, n_half), n_half), :]
        back = back + two_part_dot(mask_of((s_half, n_half), neg_row), grads)
        back_msg[to, :] = packed(back)


def edge_call(head_slot, tail_slot, rel, rows, pieces):
    edges = head_slot.shape[0]
    slots = rows.shape[0]
    part = pieces[0].shape[0]
    n_neg = slots - GROUP * GROUP * HEAD_CAP
    outs = pl.pallas_call(
        edge_kernel,
        in_specs=[vmem()] * (6 + GROUP),
        out_specs=[vmem()] * (GROUP + 1),
        out_shape=[jax.ShapeDtypeStruct((part, FULL), I16)] * GROUP
        + [jax.ShapeDtypeStruct((slots, FULL), I16)],
        scratch_shapes=[
            pltpu.VMEM((GROUP * part, FULL), BF),
            pltpu.VMEM((n_neg, FULL), BF),
            pltpu.VMEM((edges, FULL), BF),
            pltpu.VMEM((edges, FULL), BF),
            pltpu.VMEM((edges, FULL), BF),
            pltpu.VMEM((n_neg, FULL), F32),
        ],
        cost_estimate=pl.CostEstimate(flops=9 << 30, bytes_accessed=16 << 20, transcendentals=1 << 20),
        name="edge",
    )(
        head_slot[:, None],
        head_slot[None, :],
        tail_slot[:, None],
        tail_slot[None, :],
        rel,
        rows,
        *pieces,
    )
    return outs[:GROUP], outs[GROUP]


def answer_kernel(me_ref, ids_ref, *refs):
    n_ring = len(refs) - GROUP
    blocks, outs = refs[:n_ring], refs[n_ring:]
    rows = blocks[0].shape[0]
    for k in range(n_ring):
        z = lax.rem(me_ref[0] - k + n_ring, n_ring)
        mask = mask_of((rows, GROUP * TAIL_CAP), ids_ref[pl.ds(z, 1), :])
        found = dot(mask, blocks[k][...], TN).astype(BF)
        for g in range(GROUP):
            start = pl.multiple_of(z * TAIL_CAP, TAIL_CAP)
            outs[g][pl.ds(start, TAIL_CAP), :] = found[g * TAIL_CAP : (g + 1) * TAIL_CAP, :]


def answer_call(ring_me, ids, blocks):
    n_ring = len(blocks)
    return pl.pallas_call(
        answer_kernel,
        in_specs=[smem()] + [vmem()] * (1 + n_ring),
        out_specs=[vmem()] * GROUP,
        out_shape=[jax.ShapeDtypeStruct((n_ring * TAIL_CAP, FULL), BF)] * GROUP,
        cost_estimate=pl.CostEstimate(flops=1 << 30, bytes_accessed=4 << 20, transcendentals=0),
        name="answer",
    )(ring_me, ids, *blocks)


def coded_parts(src, own_ref, msgs, me, n_rep):
    @pl.loop(0, n_rep)
    def _(k):
        part = src(lax.rem(me + k, n_rep))
        pl.when(k == 0)(functools.partial(put, own_ref, part))
        code = packed(part)
        for step in range(1, n_rep):
            pl.when(k == step)(functools.partial(put, msgs[step - 1], code))


def dense_kernel(me_ref, ids_ref, *refs, n_rep):
    got, own_ref, msgs, dense = refs[:GROUP], refs[GROUP], refs[GROUP + 1 : -1], refs[-1]
    n_ring, rows, _ = dense.shape

    @pl.loop(0, n_ring)
    def _(z):
        at = pl.ds(pl.multiple_of(z * TAIL_CAP, TAIL_CAP), TAIL_CAP)
        part = [unpacked(got[g][at, :]) for g in range(GROUP)]
        mask = mask_of((rows, GROUP * TAIL_CAP), ids_ref[pl.ds(z, 1), :])
        dense[z] = two_part_dot(mask, jnp.concatenate(part, axis=0))

    quarter = rows // n_rep

    def src(q):
        start = pl.multiple_of(q * quarter, quarter)
        return dense[:, pl.ds(start, quarter), :].reshape(n_ring * quarter, FULL)

    coded_parts(src, own_ref, msgs, me_ref[0], n_rep)


def cold_kernel(me_ref, ids_ref, neg_ref, back_ref, own_ref, *refs, n_rep):
    n_src, per, _ = back_ref.shape
    msgs, flat = refs[:-1], refs[-1]
    quarter = own_ref.shape[0]
    back = unpacked(back_ref[...])
    negs = per - HEAD_CAP
    neg_sum = jnp.sum(back[:, HEAD_CAP:, :], axis=0)
    flat[...] = back.reshape(n_src * per, FULL).astype(BF)
    hi = neg_sum.astype(BF)
    rest = neg_sum - hi.astype(F32)

    def src(q):
        mask = mask_of((quarter, n_src * per), ids_ref[...], q * quarter)
        neg_mask = mask_of((quarter, negs), neg_ref[...], q * quarter)
        return dot(mask, flat[...], MM) + dot(neg_mask, hi, MM) + two_part_dot(neg_mask, rest)

    coded_parts(src, own_ref, msgs, me_ref[0], n_rep)


def smem():
    return pl.BlockSpec(memory_space=pltpu.SMEM)


def vmem():
    return pl.BlockSpec(memory_space=pltpu.VMEM)


def parts_call(kernel, me, operands, rows, scratch, n_rep):
    return pl.pallas_call(
        functools.partial(kernel, n_rep=n_rep),
        in_specs=[smem()] + [vmem()] * len(operands),
        out_specs=[vmem()] * n_rep,
        out_shape=[jax.ShapeDtypeStruct((rows, FULL), F32)]
        + [jax.ShapeDtypeStruct((rows, FULL), I16)] * (n_rep - 1),
        scratch_shapes=[scratch],
        cost_estimate=pl.CostEstimate(flops=4 << 30, bytes_accessed=8 << 20, transcendentals=0),
    )(me, *operands)


def shift(x, step, n_rep):
    return lax.ppermute(x, "rep", [(i, (i + step) % n_rep) for i in range(n_rep)])


def ring_shift(x, step, n_table):
    return lax.ppermute(x, "table", [(i, (i + step * GROUP) % n_table) for i in range(n_table)])


def near_swap(x, other, n_table):
    return lax.ppermute(x, "table", [(i, i ^ other) for i in range(n_table)])


def sum_kernel(own_ref, *refs):
    got, out_ref = refs[:-1], refs[-1]
    total = own_ref[...]
    for part in got:
        total = total + unpacked(part[...])
    out_ref[...] = packed(total) if out_ref.dtype == I16 else total


def sum_call(own, got, dtype):
    return pl.pallas_call(
        sum_kernel,
        in_specs=[vmem()] * (1 + len(got)),
        out_specs=vmem(),
        out_shape=jax.ShapeDtypeStruct(own.shape, dtype),
    )(own, *got)


def update_kernel(me_ref, table_ref, state_ref, *refs):
    parts, table_out, state_out = refs[:-2], refs[-2], refs[-1]
    n_rep = len(parts)
    half = table_ref.shape[0] // 2
    for k in range(n_rep):
        quarter = parts[k].shape[0]
        q = lax.rem(me_ref[0] - k + n_rep, n_rep)
        at = pl.ds(pl.multiple_of(q * quarter, quarter), quarter)
        grad = unpacked(parts[k][...]).T
        grad = jnp.concatenate([grad[:half], grad[HALF : HALF + half]], axis=0)
        state = state_ref[:, at] + jnp.sum(grad * grad, axis=0, keepdims=True) / (2 * half)
        state_out[:, at] = state
        table_out[:, at] = table_ref[:, at] - learn_rate * grad / jnp.sqrt(state)


def cold_update(me, table, state, parts):
    rows, width = table.shape
    new_table, new_state = pl.pallas_call(
        update_kernel,
        in_specs=[smem()] + [vmem()] * (2 + len(parts)),
        out_specs=[vmem()] * 2,
        out_shape=[
            jax.ShapeDtypeStruct((width, rows), F32),
            jax.ShapeDtypeStruct((1, rows), F32),
        ],
        name="update",
    )(me, table.T, state[None, :], *parts)
    return new_table.T, new_state[0]


def pick_kernel(ids_ref, table_ref, out_ref):
    rows = table_ref.shape[0]
    slots = out_ref.shape[0]
    step = 512

    @pl.loop(0, slots // step)
    def _(c):
        at = pl.ds(pl.multiple_of(c * step, step), step)
        out_ref[at, :] = dot(mask_of((rows, step), ids_ref[:, at]), table_ref[...], TN).astype(BF)


def pick_call(ids, table):
    slots = ids.shape[1]
    return pl.pallas_call(
        pick_kernel,
        in_specs=[vmem()] * 2,
        out_specs=vmem(),
        out_shape=jax.ShapeDtypeStruct((slots, FULL), BF),
        cost_estimate=pl.CostEstimate(flops=2 << 30, bytes_accessed=3 << 20, transcendentals=0),
        name="pick",
    )(ids, table)


def adagrad(weights, state, grad):
    new_state = state + jnp.mean(grad * grad, axis=1)
    return (weights - learn_rate * grad / jnp.sqrt(new_state)[:, None], new_state)


def per_device(
    cold_table,
    cold_state,
    hot_table,
    hot_state,
    relations,
    head_owner,
    head_row,
    edge_rel,
    edge_tail,
    neg_ids,
):
    n_table = lax.axis_size("table")
    n_rep = lax.axis_size("rep")
    n_ring = n_table // GROUP
    edges = head_row.shape[0]
    width = cold_table.shape[1]
    cold_rows = cold_table.shape[0]
    hot_rows = hot_table.shape[0]
    negs = neg_ids.shape[1]
    near = [[z * GROUP + g for g in range(GROUP)] for z in range(n_ring)]
    far = [[z * GROUP + g for z in range(n_ring)] for g in range(GROUP)]

    per = HEAD_CAP + negs
    me = lax.axis_index("rep").astype(I32).reshape(1)

    place = lax.axis_index("table").astype(I32)
    ring_me, near_me = (place // GROUP).reshape(1), place % GROUP

    hot_bf = widen(hot_table.astype(BF))
    blocks = [hot_bf]
    for k in range(1, n_ring):
        blocks.append(ring_shift(hot_bf, k, n_table))
    cold_bf = widen(cold_table.astype(BF))

    owner_hot = one_hot(head_owner[:, 0], n_table)
    row = lax.broadcasted_iota(jnp.int32, (edges, edges), 0)
    col = lax.broadcasted_iota(jnp.int32, (edges, edges), 1)
    before = dot((col < row).astype(BF), owner_hot, ((1,), (0,)))
    rank = jnp.sum(before * owner_hot.astype(F32), axis=1).astype(jnp.int32)
    head_slot = head_owner[:, 0] * per + rank

    block = edge_tail // hot_rows
    within = edge_tail % hot_rows
    block_hot = one_hot(block, n_table)
    within_hot = one_hot(within, hot_rows)
    present = (dot(block_hot, within_hot, ((0,), (0,))) > 0.5).astype(BF)
    prow = lax.broadcasted_iota(jnp.int32, (hot_rows, hot_rows), 0)
    pcol = lax.broadcasted_iota(jnp.int32, (hot_rows, hot_rows), 1)
    ranks = dot(present, (prow < pcol).astype(BF), ((1,), (0,)))
    rank_of = dot(block_hot, ranks.astype(BF), ((1,), (0,)))
    tail_rank = jnp.sum(rank_of * within_hot.astype(F32), axis=1).astype(jnp.int32)
    z_of, g_of = block // GROUP, block % GROUP
    tail_slot = ((g_of ^ near_me) * n_ring + z_of) * TAIL_CAP + tail_rank
    slot_iota = lax.broadcasted_iota(jnp.int32, (n_table, hot_rows, TAIL_CAP), 2)
    match = (ranks.astype(jnp.int32)[:, :, None] == slot_iota) & (present > 0.5)[:, :, None]
    row_iota = lax.broadcasted_iota(jnp.int32, (n_table, hot_rows, TAIL_CAP), 1) + 1
    slot_rows = jnp.sum(jnp.where(match, row_iota, 0), axis=1) - 1
    slot_rows = slot_rows.reshape(n_ring, GROUP, TAIL_CAP).transpose(1, 0, 2)

    wanted = jnp.zeros((n_table * per,), I32).at[head_slot].set(head_row).reshape(n_table, per)
    wanted = lax.all_to_all(wanted[:, :HEAD_CAP], "table", 0, 0)
    dense_rows = lax.all_to_all(
        slot_rows.reshape(GROUP, n_ring * TAIL_CAP), "table", 0, 0, axis_index_groups=near
    )
    dense_ids = dense_rows.reshape(GROUP, n_ring, TAIL_CAP)[jnp.arange(GROUP) ^ near_me]
    dense_ids = dense_ids.transpose(1, 0, 2).reshape(n_ring, GROUP * TAIL_CAP)
    own_negs = jnp.broadcast_to(neg_ids[0][None, :], (n_table, negs))
    asked = jnp.concatenate([wanted, own_negs], axis=1)
    head_ids = jnp.concatenate([wanted, jnp.full((n_table, negs), -1, I32)], axis=1)
    picked = pick_call(asked.reshape(1, n_table * per), cold_bf)
    rows = lax.all_to_all(picked.reshape(n_table, per, FULL), "table", 0, 0)
    relation = widen(relations[edge_rel])
    found = answer_call(ring_me, dense_ids, blocks)
    pieces = [found[0]] + [near_swap(found[g], g, n_table) for g in range(1, GROUP)]
    tail_msgs, back_msg = edge_call(
        head_slot, tail_slot, relation, rows.reshape(n_table * per, FULL), pieces
    )

    back = lax.all_to_all(back_msg.reshape(n_table, per, FULL), "table", 0, 0)
    tail_got = [tail_msgs[0]]
    for g in range(1, GROUP):
        tail_got.append(near_swap(tail_msgs[g], g, n_table))

    quarter = hot_rows // n_rep
    hot_own, *hot_msg = parts_call(
        dense_kernel,
        me,
        (dense_ids, *tail_got),
        n_ring * quarter,
        pltpu.VMEM((n_ring, hot_rows, FULL), F32),
        n_rep,
    )
    hot_got = [shift(hot_msg[k - 1], k, n_rep) for k in range(1, n_rep)]
    cold_own, *cold_msg = parts_call(
        cold_kernel,
        me,
        (head_ids.reshape(1, n_table * per), neg_ids, back),
        cold_rows // n_rep,
        pltpu.VMEM((n_table * per, FULL), BF),
        n_rep,
    )
    cold_got = []
    for k in range(1, n_rep):
        cold_got.append(shift(cold_msg[k - 1], k, n_rep))
    hot_own, _ = lax.optimization_barrier((hot_own, cold_own))
    hot_part = sum_call(hot_own, hot_got, F32)
    hot_rows_got = lax.all_to_all(
        hot_part.reshape(n_ring, quarter, FULL), "table", 0, 0, axis_index_groups=far
    )
    cold_part = sum_call(cold_own, cold_got, I16)
    cold_parts = [cold_part] + [shift(cold_part, k, n_rep) for k in range(1, n_rep)]
    hot_sum = jnp.sum(hot_rows_got, axis=0)
    new_cold_table, new_cold_state = cold_update(me, cold_table, cold_state, cold_parts)

    hot_parts = [hot_sum]
    for k in range(1, n_rep):
        hot_parts.append(shift(hot_sum, k, n_rep))
    hot_total = jnp.zeros((n_rep, quarter, FULL), F32)
    for k, part in enumerate(hot_parts):
        hot_total = lax.dynamic_update_index_in_dim(
            hot_total, part, lax.rem(me[0] - k + n_rep, n_rep), 0
        )
    hot_total = narrow(hot_total.reshape(hot_rows, FULL), width)
    new_hot_table, new_hot_state = adagrad(hot_table, hot_state, hot_total)
    return (new_cold_table, new_cold_state, new_hot_table, new_hot_state)


def solution(mesh):
    in_specs = (
        P("table", None),
        P("table"),
        P("table", None),
        P("table"),
        P(),
        P(("rep", "table"), None),
        P(("rep", "table")),
        P(("rep", "table")),
        P(("rep", "table")),
        P("rep", "table"),
    )
    out_specs = (P("table", None), P("table"), P("table", None), P("table"))

    return jax.shard_map(
        per_device, mesh=mesh, in_specs=in_specs, out_specs=out_specs, check_vma=False
    )
```

```python
import functools
import jax
import jax.numpy as jnp
from jax import lax
from jax.experimental import pallas as pl
from jax.experimental.pallas import tpu as pltpu
from jax.sharding import PartitionSpec as P


learn_rate = 0.5
HEAD_CAP = 16
TAIL_CAP = 32
GROUP = 8
HALF = 256
FULL = 2 * HALF

BF = jnp.bfloat16
I16 = jnp.int16
F32 = jnp.float32
I32 = jnp.int32


def dot(a, b, dims):
    return lax.dot_general(a, b, (dims, ((), ())), preferred_element_type=F32)


MM = ((1,), (0,))
NT = ((1,), (1,))
TN = ((0,), (0,))


def one_hot(ids, count):
    return (ids[:, None] == lax.broadcasted_iota(I32, (1, count), 1)).astype(BF)


def widen(rows):
    half = rows.shape[-1] // 2
    pad = [(0, 0)] * (rows.ndim - 1) + [(0, HALF - half)]
    return jnp.concatenate([jnp.pad(rows[..., :half], pad), jnp.pad(rows[..., half:], pad)], -1)


def narrow(rows, width):
    half = width // 2
    return jnp.concatenate([rows[..., :half], rows[..., HALF : HALF + half]], -1)


def mask_of(shape, ids_row, base=0):
    return (lax.broadcasted_iota(I32, shape, 0) + base == ids_row).astype(BF)


def two_part_dot(mask, x, dims=MM):
    hi = x.astype(BF)
    lo = (x - hi.astype(F32)).astype(BF)
    return dot(mask, hi, dims) + dot(mask, lo, dims)


def packed(x):
    peak = jnp.max(jnp.abs(x), axis=-1, keepdims=True)
    power = jnp.floor(jnp.log(jnp.maximum(peak, 1e-30)) * 1.4426950408889634)
    code = jnp.round(x * jnp.exp2(14.0 - power))
    lane = lax.broadcasted_iota(I32, x.shape, x.ndim - 1)
    code = jnp.where(lane >= FULL - 8, power, jnp.clip(code, -32767.0, 32767.0))
    return code.astype(I32).astype(I16)


def unpacked(code):
    x = code.astype(F32)
    lane = lax.broadcasted_iota(I32, x.shape, x.ndim - 1)
    scale = jnp.exp2(x[..., FULL - 1 :] - 14.0)
    return jnp.where(lane >= FULL - 8, 0.0, x * scale)


def with_rel(rel, v):
    v_re, v_im, r_re, r_im = v[:, :HALF], v[:, HALF:], rel[:, :HALF], rel[:, HALF:]
    return jnp.concatenate([v_re * r_re - v_im * r_im, v_re * r_im + v_im * r_re], axis=1)


def against_rel(rel, v):
    v_re, v_im, r_re, r_im = v[:, :HALF], v[:, HALF:], rel[:, :HALF], rel[:, HALF:]
    return jnp.concatenate([r_re * v_re + r_im * v_im, r_re * v_im - r_im * v_re], axis=1)


def put(ref, value):
    ref[...] = value


def edge_kernel(slot_col, slot_row, tail_col, tail_row, rel_ref, rows_ref, *refs):
    pieces, (same_msg, other_msg, back_msg) = refs[:5], refs[5:8]
    found, negs, hi_buf, lo_buf, head_buf, neg_buf = refs[8:]
    edges = slot_col.shape[0]
    slots = rows_ref.shape[0]
    part = found.shape[0] // GROUP
    per = slots // (GROUP * GROUP)
    n_neg = negs.shape[0]
    found[:part, :] = pieces[0][:part, :]
    found[part : 2 * part, :] = pieces[1][:part, :]
    for y in range(1, GROUP // 2):
        found[2 * y * part : 2 * (y + 1) * part, :] = pieces[y + 1][...]
    halves = 2
    e_half, s_half, n_half = edges // halves, slots // halves, n_neg // halves
    j = lax.broadcasted_iota(I32, (n_half, 1), 0)
    neg_col = (j >> 3) * per + HEAD_CAP + (j & 7)
    j = lax.broadcasted_iota(I32, (1, n_half), 1)
    neg_row = (j >> 3) * per + HEAD_CAP + (j & 7)

    @pl.loop(0, halves)
    def _(c):
        at = pl.ds(pl.multiple_of(c * s_half, s_half), s_half)
        pick = (neg_col == lax.broadcasted_iota(I32, (n_half, s_half), 1)).astype(BF)
        to = pl.ds(pl.multiple_of(c * n_half, n_half), n_half)
        negs[to, :] = dot(pick, rows_ref[at, :], MM).astype(BF)

    neg_buf[...] = jnp.zeros_like(neg_buf)

    @pl.loop(0, halves)
    def _(h):
        at = pl.ds(pl.multiple_of(h * e_half, e_half), e_half)
        rel = rel_ref[at, :]
        pick = tail_col[at, :] == lax.broadcasted_iota(I32, (e_half, GROUP * part), 1)
        tail_f = dot(pick.astype(BF), found[...], MM)
        pick = slot_col[at, :] == lax.broadcasted_iota(I32, (e_half, slots), 1)
        head_f = dot(pick.astype(BF), rows_ref[...], MM)
        negatives = negs[...]
        queries = with_rel(rel, head_f)
        probes = against_rel(rel, tail_f)
        positive = jnp.sum(queries * tail_f, axis=1, keepdims=True)
        query_b = queries.astype(BF)
        probe_b = probes.astype(BF)
        pos_weight = -jax.nn.sigmoid(-positive)
        tail_weight = jax.nn.sigmoid(dot(query_b, negatives, NT)).astype(BF)
        head_weight = jax.nn.sigmoid(dot(probe_b, negatives, NT)).astype(BF)
        tail_mix = dot(tail_weight, negatives, MM)
        head_mix = dot(head_weight, negatives, MM)
        head_buf[at, :] = against_rel(rel, pos_weight * tail_f + tail_mix).astype(BF)
        tail_grad = with_rel(rel, pos_weight * head_f + head_mix)
        grad_hi = tail_grad.astype(BF)
        hi_buf[at, :] = grad_hi
        lo_buf[at, :] = (tail_grad - grad_hi.astype(F32)).astype(BF)
        neg_buf[...] += dot(tail_weight, query_b, TN) + dot(head_weight, probe_b, TN)

    @pl.loop(0, GROUP)
    def _(k):
        mask = mask_of((part, edges), tail_row[...], k * part)
        code = packed(dot(mask, hi_buf[...], MM) + dot(mask, lo_buf[...], MM))
        at = pl.ds(pl.multiple_of((k >> 1) * part, part), part)
        pl.when((k & 1) == 0)(functools.partial(put, same_msg.at[at], code))
        pl.when((k & 1) == 1)(functools.partial(put, other_msg.at[at], code))

    @pl.loop(0, halves)
    def _(c):
        to = pl.ds(pl.multiple_of(c * s_half, s_half), s_half)
        back = dot(mask_of((s_half, edges), slot_row[...], c * s_half), head_buf[...], MM)
        grads = neg_buf[pl.ds(pl.multiple_of(c * n_half, n_half), n_half), :]
        back = back + two_part_dot(mask_of((s_half, n_half), neg_row), grads)
        back_msg[to, :] = packed(back)


def edge_call(head_slot, tail_slot, rel, rows, pieces):
    edges = head_slot.shape[0]
    slots = rows.shape[0]
    part = pieces[1].shape[0] * 2 // GROUP
    n_neg = slots - GROUP * GROUP * HEAD_CAP
    outs = pl.pallas_call(
        edge_kernel,
        in_specs=[vmem()] * (6 + len(pieces)),
        out_specs=[vmem()] * 3,
        out_shape=[jax.ShapeDtypeStruct((GROUP // 2 * part, FULL), I16)] * 2
        + [jax.ShapeDtypeStruct((slots, FULL), I16)],
        scratch_shapes=[
            pltpu.VMEM((GROUP * part, FULL), BF),
            pltpu.VMEM((n_neg, FULL), BF),
            pltpu.VMEM((edges, FULL), BF),
            pltpu.VMEM((edges, FULL), BF),
            pltpu.VMEM((edges, FULL), BF),
            pltpu.VMEM((n_neg, FULL), F32),
        ],
        cost_estimate=pl.CostEstimate(flops=9 << 30, bytes_accessed=16 << 20, transcendentals=1 << 20),
        name="edge",
    )(
        head_slot[:, None],
        head_slot[None, :],
        tail_slot[:, None],
        tail_slot[None, :],
        rel,
        rows,
        *pieces,
    )
    return outs


def answer_kernel(me_ref, ids_ref, here, behind, ahead, same_out, other_out):
    n_ring = ids_ref.shape[0]
    rows = here.shape[0] // 3
    places = ((here, 1), (here, 0), (behind, 2), (behind, 1), (behind, 0), (ahead, 1), (ahead, 0), (here, 2))
    for k, (ref, i) in enumerate(places):
        z = lax.rem(me_ref[0] - k + n_ring, n_ring)
        mask = mask_of((rows, GROUP * TAIL_CAP), ids_ref[pl.ds(z, 1), :])
        found = dot(mask, ref[i * rows : (i + 1) * rows, :], TN).astype(BF)
        for g in range(GROUP):
            start = pl.multiple_of((g // 2) * n_ring * TAIL_CAP + z * TAIL_CAP, TAIL_CAP)
            out = other_out if g % 2 else same_out
            out[pl.ds(start, TAIL_CAP), :] = found[g * TAIL_CAP : (g + 1) * TAIL_CAP, :]


def answer_call(ring_me, ids, blocks):
    n_ring = ids.shape[0]
    out = jax.ShapeDtypeStruct((GROUP // 2 * n_ring * TAIL_CAP, FULL), BF)
    return pl.pallas_call(
        answer_kernel,
        in_specs=[smem()] + [vmem()] * (1 + len(blocks)),
        out_specs=[vmem()] * 2,
        out_shape=[out] * 2,
        cost_estimate=pl.CostEstimate(flops=1 << 30, bytes_accessed=4 << 20, transcendentals=0),
        name="answer",
    )(ring_me, ids, *blocks)


def coded_parts(src, own_ref, msgs, me, n_rep):
    @pl.loop(0, n_rep)
    def _(k):
        part = src(lax.rem(me + k, n_rep))
        pl.when(k == 0)(functools.partial(put, own_ref, part))
        code = packed(part)
        for step in range(1, n_rep):
            pl.when(k == step)(functools.partial(put, msgs[step - 1], code))


def dense_kernel(me_ref, ids_ref, *refs, n_rep):
    got, own_ref, msgs, dense = refs[:5], refs[5], refs[6:-1], refs[-1]
    n_ring, rows, _ = dense.shape

    @pl.loop(0, n_ring)
    def _(z):
        at = pl.ds(pl.multiple_of(z * TAIL_CAP, TAIL_CAP), TAIL_CAP)
        then = pl.ds(pl.multiple_of((n_ring + z) * TAIL_CAP, TAIL_CAP), TAIL_CAP)
        part = [got[0][at, :], got[1][at, :]]
        for pair in got[2:]:
            part += [pair[at, :], pair[then, :]]
        part = [unpacked(code) for code in part]
        mask = mask_of((rows, GROUP * TAIL_CAP), ids_ref[pl.ds(z, 1), :])
        dense[z] = two_part_dot(mask, jnp.concatenate(part, axis=0))

    quarter = rows // n_rep

    def src(q):
        start = pl.multiple_of(q * quarter, quarter)
        return dense[:, pl.ds(start, quarter), :].reshape(n_ring * quarter, FULL)

    coded_parts(src, own_ref, msgs, me_ref[0], n_rep)


def cold_kernel(me_ref, ids_ref, neg_ref, back_ref, own_ref, *refs, n_rep):
    n_src, per, _ = back_ref.shape
    msgs, flat = refs[:-1], refs[-1]
    quarter = own_ref.shape[0]
    back = unpacked(back_ref[...])
    negs = per - HEAD_CAP
    neg_sum = jnp.sum(back[:, HEAD_CAP:, :], axis=0)
    flat[...] = back.reshape(n_src * per, FULL).astype(BF)
    hi = neg_sum.astype(BF)
    rest = neg_sum - hi.astype(F32)

    def src(q):
        mask = mask_of((quarter, n_src * per), ids_ref[...], q * quarter)
        neg_mask = mask_of((quarter, negs), neg_ref[...], q * quarter)
        return dot(mask, flat[...], MM) + dot(neg_mask, hi, MM) + two_part_dot(neg_mask, rest)

    coded_parts(src, own_ref, msgs, me_ref[0], n_rep)


def smem():
    return pl.BlockSpec(memory_space=pltpu.SMEM)


def vmem():
    return pl.BlockSpec(memory_space=pltpu.VMEM)


def parts_call(kernel, me, operands, rows, scratch, n_rep):
    return pl.pallas_call(
        functools.partial(kernel, n_rep=n_rep),
        in_specs=[smem()] + [vmem()] * len(operands),
        out_specs=[vmem()] * n_rep,
        out_shape=[jax.ShapeDtypeStruct((rows, FULL), F32)]
        + [jax.ShapeDtypeStruct((rows, FULL), I16)] * (n_rep - 1),
        scratch_shapes=[scratch],
        cost_estimate=pl.CostEstimate(flops=4 << 30, bytes_accessed=8 << 20, transcendentals=0),
    )(me, *operands)


def shift(x, step, n_rep):
    return lax.ppermute(x, "rep", [(i, (i + step) % n_rep) for i in range(n_rep)])


def ring_shift(x, step, n_table):
    return lax.ppermute(x, "table", [(i, (i + step * GROUP) % n_table) for i in range(n_table)])


def near_swap(x, other, n_table):
    return lax.ppermute(x, "table", [(i, i ^ other) for i in range(n_table)])


def near_exchange(same, other, n_table):
    swapped = near_swap(other, 1, n_table)
    got = [same, swapped]
    size = same.shape[0] // (GROUP // 2)
    for y in range(1, GROUP // 2):
        at = slice(y * size, (y + 1) * size)
        got.append(near_swap(jnp.concatenate([same[at], swapped[at]]), 2 * y, n_table))
    return got


def sum_kernel(own_ref, *refs):
    got, out_ref = refs[:-1], refs[-1]
    total = own_ref[...]
    for part in got:
        total = total + unpacked(part[...])
    out_ref[...] = packed(total) if out_ref.dtype == I16 else total


def sum_call(own, got, dtype):
    return pl.pallas_call(
        sum_kernel,
        in_specs=[vmem()] * (1 + len(got)),
        out_specs=vmem(),
        out_shape=jax.ShapeDtypeStruct(own.shape, dtype),
    )(own, *got)


def update_kernel(me_ref, table_ref, state_ref, *refs):
    parts, table_out, state_out = refs[:-2], refs[-2], refs[-1]
    n_rep = len(parts)
    half = table_ref.shape[0] // 2
    for k in range(n_rep):
        quarter = parts[k].shape[0]
        q = lax.rem(me_ref[0] - k + n_rep, n_rep)
        at = pl.ds(pl.multiple_of(q * quarter, quarter), quarter)
        grad = unpacked(parts[k][...]).T
        grad = jnp.concatenate([grad[:half], grad[HALF : HALF + half]], axis=0)
        state = state_ref[:, at] + jnp.sum(grad * grad, axis=0, keepdims=True) / (2 * half)
        state_out[:, at] = state
        table_out[:, at] = table_ref[:, at] - learn_rate * grad / jnp.sqrt(state)


def cold_update(me, table, state, parts):
    rows, width = table.shape
    new_table, new_state = pl.pallas_call(
        update_kernel,
        in_specs=[smem()] + [vmem()] * (2 + len(parts)),
        out_specs=[vmem()] * 2,
        out_shape=[
            jax.ShapeDtypeStruct((width, rows), F32),
            jax.ShapeDtypeStruct((1, rows), F32),
        ],
        name="update",
    )(me, table.T, state[None, :], *parts)
    return new_table.T, new_state[0]


def pick_kernel(ids_ref, table_ref, out_ref):
    rows = table_ref.shape[0]
    slots = out_ref.shape[0]
    step = 512

    @pl.loop(0, slots // step)
    def _(c):
        at = pl.ds(pl.multiple_of(c * step, step), step)
        out_ref[at, :] = dot(mask_of((rows, step), ids_ref[:, at]), table_ref[...], TN).astype(BF)


def pick_call(ids, table):
    slots = ids.shape[1]
    return pl.pallas_call(
        pick_kernel,
        in_specs=[vmem()] * 2,
        out_specs=vmem(),
        out_shape=jax.ShapeDtypeStruct((slots, FULL), BF),
        cost_estimate=pl.CostEstimate(flops=2 << 30, bytes_accessed=3 << 20, transcendentals=0),
        name="pick",
    )(ids, table)


def adagrad(weights, state, grad):
    new_state = state + jnp.mean(grad * grad, axis=1)
    return (weights - learn_rate * grad / jnp.sqrt(new_state)[:, None], new_state)


def per_device(
    cold_table,
    cold_state,
    hot_table,
    hot_state,
    relations,
    head_owner,
    head_row,
    edge_rel,
    edge_tail,
    neg_ids,
):
    n_table = lax.axis_size("table")
    n_rep = lax.axis_size("rep")
    n_ring = n_table // GROUP
    edges = head_row.shape[0]
    width = cold_table.shape[1]
    cold_rows = cold_table.shape[0]
    hot_rows = hot_table.shape[0]
    negs = neg_ids.shape[1]
    near = [[z * GROUP + g for g in range(GROUP)] for z in range(n_ring)]
    far = [[z * GROUP + g for z in range(n_ring)] for g in range(GROUP)]

    per = HEAD_CAP + negs
    me = lax.axis_index("rep").astype(I32).reshape(1)

    place = lax.axis_index("table").astype(I32)
    ring_me, near_me = (place // GROUP).reshape(1), place % GROUP

    hot_bf = widen(hot_table.astype(BF))
    before_us = ring_shift(hot_bf, 1, n_table)
    after_us = ring_shift(hot_bf, n_ring - 1, n_table)
    here = jnp.concatenate([before_us, hot_bf, after_us])
    behind = ring_shift(here, 3, n_table)
    ahead = ring_shift(here, n_ring - 3, n_table)
    cold_bf = widen(cold_table.astype(BF))

    owner_hot = one_hot(head_owner[:, 0], n_table)
    row = lax.broadcasted_iota(jnp.int32, (edges, edges), 0)
    col = lax.broadcasted_iota(jnp.int32, (edges, edges), 1)
    before = dot((col < row).astype(BF), owner_hot, ((1,), (0,)))
    rank = jnp.sum(before * owner_hot.astype(F32), axis=1).astype(jnp.int32)
    head_slot = head_owner[:, 0] * per + rank

    block = edge_tail // hot_rows
    within = edge_tail % hot_rows
    block_hot = one_hot(block, n_table)
    within_hot = one_hot(within, hot_rows)
    present = (dot(block_hot, within_hot, ((0,), (0,))) > 0.5).astype(BF)
    prow = lax.broadcasted_iota(jnp.int32, (hot_rows, hot_rows), 0)
    pcol = lax.broadcasted_iota(jnp.int32, (hot_rows, hot_rows), 1)
    ranks = dot(present, (prow < pcol).astype(BF), ((1,), (0,)))
    rank_of = dot(block_hot, ranks.astype(BF), ((1,), (0,)))
    tail_rank = jnp.sum(rank_of * within_hot.astype(F32), axis=1).astype(jnp.int32)
    z_of, g_of = block // GROUP, block % GROUP
    tail_slot = ((g_of ^ near_me) * n_ring + z_of) * TAIL_CAP + tail_rank
    slot_iota = lax.broadcasted_iota(jnp.int32, (n_table, hot_rows, TAIL_CAP), 2)
    match = (ranks.astype(jnp.int32)[:, :, None] == slot_iota) & (present > 0.5)[:, :, None]
    row_iota = lax.broadcasted_iota(jnp.int32, (n_table, hot_rows, TAIL_CAP), 1) + 1
    slot_rows = jnp.sum(jnp.where(match, row_iota, 0), axis=1) - 1
    slot_rows = slot_rows.reshape(n_ring, GROUP, TAIL_CAP).transpose(1, 0, 2)

    wanted = jnp.zeros((n_table * per,), I32).at[head_slot].set(head_row).reshape(n_table, per)
    wanted = lax.all_to_all(wanted[:, :HEAD_CAP], "table", 0, 0)
    dense_rows = lax.all_to_all(
        slot_rows.reshape(GROUP, n_ring * TAIL_CAP), "table", 0, 0, axis_index_groups=near
    )
    dense_ids = dense_rows.reshape(GROUP, n_ring, TAIL_CAP)[jnp.arange(GROUP) ^ near_me]
    dense_ids = dense_ids.transpose(1, 0, 2).reshape(n_ring, GROUP * TAIL_CAP)
    own_negs = jnp.broadcast_to(neg_ids[0][None, :], (n_table, negs))
    asked = jnp.concatenate([wanted, own_negs], axis=1)
    head_ids = jnp.concatenate([wanted, jnp.full((n_table, negs), -1, I32)], axis=1)
    picked = pick_call(asked.reshape(1, n_table * per), cold_bf)
    rows = lax.all_to_all(picked.reshape(n_table, per, FULL), "table", 0, 0)
    relation = widen(relations[edge_rel])
    found = answer_call(ring_me, dense_ids, (here, behind, ahead))
    pieces = near_exchange(*found, n_table)
    same_msg, other_msg, back_msg = edge_call(
        head_slot, tail_slot, relation, rows.reshape(n_table * per, FULL), pieces
    )

    back = lax.all_to_all(back_msg.reshape(n_table, per, FULL), "table", 0, 0)
    tail_got = near_exchange(same_msg, other_msg, n_table)

    quarter = hot_rows // n_rep
    hot_own, *hot_msg = parts_call(
        dense_kernel,
        me,
        (dense_ids, *tail_got),
        n_ring * quarter,
        pltpu.VMEM((n_ring, hot_rows, FULL), F32),
        n_rep,
    )
    hot_got = [shift(hot_msg[k - 1], k, n_rep) for k in range(1, n_rep)]
    cold_own, *cold_msg = parts_call(
        cold_kernel,
        me,
        (head_ids.reshape(1, n_table * per), neg_ids, back),
        cold_rows // n_rep,
        pltpu.VMEM((n_table * per, FULL), BF),
        n_rep,
    )
    cold_got = []
    for k in range(1, n_rep):
        cold_got.append(shift(cold_msg[k - 1], k, n_rep))
    hot_own, _ = lax.optimization_barrier((hot_own, cold_own))
    hot_part = sum_call(hot_own, hot_got, F32)
    hot_rows_got = lax.all_to_all(
        hot_part.reshape(n_ring, quarter, FULL), "table", 0, 0, axis_index_groups=far
    )
    cold_part = sum_call(cold_own, cold_got, I16)
    cold_parts = [cold_part] + [shift(cold_part, k, n_rep) for k in range(1, n_rep)]
    hot_sum = jnp.sum(hot_rows_got, axis=0)
    new_cold_table, new_cold_state = cold_update(me, cold_table, cold_state, cold_parts)

    hot_parts = [hot_sum]
    for k in range(1, n_rep):
        hot_parts.append(shift(hot_sum, k, n_rep))
    hot_total = jnp.zeros((n_rep, quarter, FULL), F32)
    for k, part in enumerate(hot_parts):
        hot_total = lax.dynamic_update_index_in_dim(
            hot_total, part, lax.rem(me[0] - k + n_rep, n_rep), 0
        )
    hot_total = narrow(hot_total.reshape(hot_rows, FULL), width)
    new_hot_table, new_hot_state = adagrad(hot_table, hot_state, hot_total)
    return (new_cold_table, new_cold_state, new_hot_table, new_hot_state)


def solution(mesh):
    in_specs = (
        P("table", None),
        P("table"),
        P("table", None),
        P("table"),
        P(),
        P(("rep", "table"), None),
        P(("rep", "table")),
        P(("rep", "table")),
        P(("rep", "table")),
        P("rep", "table"),
    )
    out_specs = (P("table", None), P("table"), P("table", None), P("table"))

    return jax.shard_map(
        per_device, mesh=mesh, in_specs=in_specs, out_specs=out_specs, check_vma=False
    )
```

```python
import functools
import jax
import jax.numpy as jnp
from jax import lax
from jax.experimental import pallas as pl
from jax.experimental.pallas import tpu as pltpu
from jax.sharding import PartitionSpec as P


learn_rate = 0.5
HEAD_CAP = 16
TAIL_CAP = 32
GROUP = 8
HALF = 256
FULL = 2 * HALF

BF = jnp.bfloat16
I16 = jnp.int16
F32 = jnp.float32
I32 = jnp.int32


def dot(a, b, dims):
    return lax.dot_general(a, b, (dims, ((), ())), preferred_element_type=F32)


MM = ((1,), (0,))
NT = ((1,), (1,))
TN = ((0,), (0,))


def one_hot(ids, count):
    return (ids[:, None] == lax.broadcasted_iota(I32, (1, count), 1)).astype(BF)


def widen(rows):
    half = rows.shape[-1] // 2
    pad = [(0, 0)] * (rows.ndim - 1) + [(0, HALF - half)]
    return jnp.concatenate([jnp.pad(rows[..., :half], pad), jnp.pad(rows[..., half:], pad)], -1)


def narrow(rows, width):
    half = width // 2
    return jnp.concatenate([rows[..., :half], rows[..., HALF : HALF + half]], -1)


def mask_of(shape, ids_row, base=0):
    return (lax.broadcasted_iota(I32, shape, 0) + base == ids_row).astype(BF)


def two_part_dot(mask, x, dims=MM):
    hi = x.astype(BF)
    lo = (x - hi.astype(F32)).astype(BF)
    return dot(mask, hi, dims) + dot(mask, lo, dims)


def packed(x):
    peak = jnp.max(jnp.abs(x), axis=-1, keepdims=True)
    power = jnp.floor(jnp.log(jnp.maximum(peak, 1e-30)) * 1.4426950408889634)
    code = jnp.round(x * jnp.exp2(14.0 - power))
    lane = lax.broadcasted_iota(I32, x.shape, x.ndim - 1)
    code = jnp.where(lane >= FULL - 8, power, jnp.clip(code, -32767.0, 32767.0))
    return code.astype(I32).astype(I16)


def unpacked(code):
    x = code.astype(F32)
    lane = lax.broadcasted_iota(I32, x.shape, x.ndim - 1)
    scale = jnp.exp2(x[..., FULL - 1 :] - 14.0)
    return jnp.where(lane >= FULL - 8, 0.0, x * scale)


POWER_ROWS = 16


def across(x, width):
    half = width // 2
    x = x.T
    return jnp.concatenate([x[:half], x[HALF : HALF + half]], axis=0)


def packed_across(x):
    peak = jnp.max(jnp.abs(x), axis=0, keepdims=True)
    power = jnp.floor(jnp.log(jnp.maximum(peak, 1e-30)) * 1.4426950408889634)
    code = jnp.clip(jnp.round(x * jnp.exp2(14.0 - power)), -32767.0, 32767.0)
    power = jnp.broadcast_to(power, (POWER_ROWS, x.shape[1]))
    return jnp.concatenate([code, power], axis=0).astype(I32).astype(I16)


def unpacked_across(code):
    x = code.astype(F32)
    width = x.shape[0] - POWER_ROWS
    return x[:width] * jnp.exp2(x[width : width + 1] - 14.0)


def with_rel(rel, v):
    v_re, v_im, r_re, r_im = v[:, :HALF], v[:, HALF:], rel[:, :HALF], rel[:, HALF:]
    return jnp.concatenate([v_re * r_re - v_im * r_im, v_re * r_im + v_im * r_re], axis=1)


def against_rel(rel, v):
    v_re, v_im, r_re, r_im = v[:, :HALF], v[:, HALF:], rel[:, :HALF], rel[:, HALF:]
    return jnp.concatenate([r_re * v_re + r_im * v_im, r_re * v_im - r_im * v_re], axis=1)


def put(ref, value):
    ref[...] = value


def edge_kernel(slot_col, slot_row, tail_col, tail_row, rel_ref, rows_ref, *refs):
    pieces, (same_msg, other_msg, back_msg) = refs[:5], refs[5:8]
    found, negs, hi_buf, lo_buf, head_buf, neg_buf = refs[8:]
    edges = slot_col.shape[0]
    slots = rows_ref.shape[0]
    part = found.shape[0] // GROUP
    per = slots // (GROUP * GROUP)
    n_neg = negs.shape[0]
    found[:part, :] = pieces[0][:part, :]
    found[part : 2 * part, :] = pieces[1][:part, :]
    for y in range(1, GROUP // 2):
        found[2 * y * part : 2 * (y + 1) * part, :] = pieces[y + 1][...]
    halves = 2
    e_half, s_half, n_half = edges // halves, slots // halves, n_neg // halves
    j = lax.broadcasted_iota(I32, (n_half, 1), 0)
    neg_col = (j >> 3) * per + HEAD_CAP + (j & 7)
    j = lax.broadcasted_iota(I32, (1, n_half), 1)
    neg_row = (j >> 3) * per + HEAD_CAP + (j & 7)

    @pl.loop(0, halves)
    def _(c):
        at = pl.ds(pl.multiple_of(c * s_half, s_half), s_half)
        pick = (neg_col == lax.broadcasted_iota(I32, (n_half, s_half), 1)).astype(BF)
        to = pl.ds(pl.multiple_of(c * n_half, n_half), n_half)
        negs[to, :] = dot(pick, rows_ref[at, :], MM).astype(BF)

    neg_buf[...] = jnp.zeros_like(neg_buf)

    @pl.loop(0, halves)
    def _(h):
        at = pl.ds(pl.multiple_of(h * e_half, e_half), e_half)
        rel = rel_ref[at, :]
        pick = tail_col[at, :] == lax.broadcasted_iota(I32, (e_half, GROUP * part), 1)
        tail_f = dot(pick.astype(BF), found[...], MM)
        pick = slot_col[at, :] == lax.broadcasted_iota(I32, (e_half, slots), 1)
        head_f = dot(pick.astype(BF), rows_ref[...], MM)
        negatives = negs[...]
        queries = with_rel(rel, head_f)
        probes = against_rel(rel, tail_f)
        positive = jnp.sum(queries * tail_f, axis=1, keepdims=True)
        query_b = queries.astype(BF)
        probe_b = probes.astype(BF)
        pos_weight = -jax.nn.sigmoid(-positive)
        tail_weight = jax.nn.sigmoid(dot(query_b, negatives, NT)).astype(BF)
        head_weight = jax.nn.sigmoid(dot(probe_b, negatives, NT)).astype(BF)
        tail_mix = dot(tail_weight, negatives, MM)
        head_mix = dot(head_weight, negatives, MM)
        head_buf[at, :] = against_rel(rel, pos_weight * tail_f + tail_mix).astype(BF)
        tail_grad = with_rel(rel, pos_weight * head_f + head_mix)
        grad_hi = tail_grad.astype(BF)
        hi_buf[at, :] = grad_hi
        lo_buf[at, :] = (tail_grad - grad_hi.astype(F32)).astype(BF)
        neg_buf[...] += dot(tail_weight, query_b, TN) + dot(head_weight, probe_b, TN)

    @pl.loop(0, GROUP)
    def _(k):
        mask = mask_of((part, edges), tail_row[...], k * part)
        code = packed(dot(mask, hi_buf[...], MM) + dot(mask, lo_buf[...], MM))
        at = pl.ds(pl.multiple_of((k >> 1) * part, part), part)
        pl.when((k & 1) == 0)(functools.partial(put, same_msg.at[at], code))
        pl.when((k & 1) == 1)(functools.partial(put, other_msg.at[at], code))

    @pl.loop(0, halves)
    def _(c):
        to = pl.ds(pl.multiple_of(c * s_half, s_half), s_half)
        back = dot(mask_of((s_half, edges), slot_row[...], c * s_half), head_buf[...], MM)
        grads = neg_buf[pl.ds(pl.multiple_of(c * n_half, n_half), n_half), :]
        back = back + two_part_dot(mask_of((s_half, n_half), neg_row), grads)
        back_msg[to, :] = packed(back)


def edge_call(head_slot, tail_slot, rel, rows, pieces):
    edges = head_slot.shape[0]
    slots = rows.shape[0]
    part = pieces[1].shape[0] * 2 // GROUP
    n_neg = slots - GROUP * GROUP * HEAD_CAP
    outs = pl.pallas_call(
        edge_kernel,
        in_specs=[vmem()] * (6 + len(pieces)),
        out_specs=[vmem()] * 3,
        out_shape=[jax.ShapeDtypeStruct((GROUP // 2 * part, FULL), I16)] * 2
        + [jax.ShapeDtypeStruct((slots, FULL), I16)],
        scratch_shapes=[
            pltpu.VMEM((GROUP * part, FULL), BF),
            pltpu.VMEM((n_neg, FULL), BF),
            pltpu.VMEM((edges, FULL), BF),
            pltpu.VMEM((edges, FULL), BF),
            pltpu.VMEM((edges, FULL), BF),
            pltpu.VMEM((n_neg, FULL), F32),
        ],
        cost_estimate=pl.CostEstimate(flops=9 << 30, bytes_accessed=16 << 20, transcendentals=1 << 20),
        name="edge",
    )(
        head_slot[:, None],
        head_slot[None, :],
        tail_slot[:, None],
        tail_slot[None, :],
        rel,
        rows,
        *pieces,
    )
    return outs


def answer_kernel(me_ref, ids_ref, here, behind, ahead, same_out, other_out):
    n_ring = ids_ref.shape[0]
    rows = here.shape[0] // 3
    places = ((here, 1), (here, 0), (behind, 2), (behind, 1), (behind, 0), (ahead, 1), (ahead, 0), (here, 2))
    for k, (ref, i) in enumerate(places):
        z = lax.rem(me_ref[0] - k + n_ring, n_ring)
        mask = mask_of((rows, GROUP * TAIL_CAP), ids_ref[pl.ds(z, 1), :])
        found = dot(mask, ref[i * rows : (i + 1) * rows, :], TN).astype(BF)
        for g in range(GROUP):
            start = pl.multiple_of((g // 2) * n_ring * TAIL_CAP + z * TAIL_CAP, TAIL_CAP)
            out = other_out if g % 2 else same_out
            out[pl.ds(start, TAIL_CAP), :] = found[g * TAIL_CAP : (g + 1) * TAIL_CAP, :]


def answer_call(ring_me, ids, blocks):
    n_ring = ids.shape[0]
    out = jax.ShapeDtypeStruct((GROUP // 2 * n_ring * TAIL_CAP, FULL), BF)
    return pl.pallas_call(
        answer_kernel,
        in_specs=[smem()] + [vmem()] * (1 + len(blocks)),
        out_specs=[vmem()] * 2,
        out_shape=[out] * 2,
        cost_estimate=pl.CostEstimate(flops=1 << 30, bytes_accessed=4 << 20, transcendentals=0),
        name="answer",
    )(ring_me, ids, *blocks)


def coded_parts(src, own_ref, msgs, me, n_rep):
    @pl.loop(0, n_rep)
    def _(k):
        part = across(src(lax.rem(me + k, n_rep)), own_ref.shape[0])
        pl.when(k == 0)(functools.partial(put, own_ref, part))
        code = packed_across(part)
        for step in range(1, n_rep):
            pl.when(k == step)(functools.partial(put, msgs[step - 1], code))


def dense_kernel(me_ref, ids_ref, *refs, n_rep):
    got, own_ref, msgs, dense = refs[:5], refs[5], refs[6:-1], refs[-1]
    n_ring, rows, _ = dense.shape

    @pl.loop(0, n_ring)
    def _(z):
        at = pl.ds(pl.multiple_of(z * TAIL_CAP, TAIL_CAP), TAIL_CAP)
        then = pl.ds(pl.multiple_of((n_ring + z) * TAIL_CAP, TAIL_CAP), TAIL_CAP)
        part = [got[0][at, :], got[1][at, :]]
        for pair in got[2:]:
            part += [pair[at, :], pair[then, :]]
        part = [unpacked(code) for code in part]
        mask = mask_of((rows, GROUP * TAIL_CAP), ids_ref[pl.ds(z, 1), :])
        dense[z] = two_part_dot(mask, jnp.concatenate(part, axis=0))

    quarter = rows // n_rep

    def src(q):
        start = pl.multiple_of(q * quarter, quarter)
        return dense[:, pl.ds(start, quarter), :].reshape(n_ring * quarter, FULL)

    coded_parts(src, own_ref, msgs, me_ref[0], n_rep)


def cold_kernel(me_ref, ids_ref, neg_ref, back_ref, own_ref, *refs, n_rep):
    n_src, per, _ = back_ref.shape
    msgs, flat = refs[:-1], refs[-1]
    quarter = own_ref.shape[1]
    back = unpacked(back_ref[...])
    negs = per - HEAD_CAP
    neg_sum = jnp.sum(back[:, HEAD_CAP:, :], axis=0)
    flat[...] = back.reshape(n_src * per, FULL).astype(BF)
    hi = neg_sum.astype(BF)
    rest = neg_sum - hi.astype(F32)

    def src(q):
        mask = mask_of((quarter, n_src * per), ids_ref[...], q * quarter)
        neg_mask = mask_of((quarter, negs), neg_ref[...], q * quarter)
        return dot(mask, flat[...], MM) + dot(neg_mask, hi, MM) + two_part_dot(neg_mask, rest)

    coded_parts(src, own_ref, msgs, me_ref[0], n_rep)


def smem():
    return pl.BlockSpec(memory_space=pltpu.SMEM)


def vmem():
    return pl.BlockSpec(memory_space=pltpu.VMEM)


def parts_call(kernel, me, operands, width, rows, scratch, n_rep):
    return pl.pallas_call(
        functools.partial(kernel, n_rep=n_rep),
        in_specs=[smem()] + [vmem()] * len(operands),
        out_specs=[vmem()] * n_rep,
        out_shape=[jax.ShapeDtypeStruct((width, rows), F32)]
        + [jax.ShapeDtypeStruct((width + POWER_ROWS, rows), I16)] * (n_rep - 1),
        scratch_shapes=[scratch],
        cost_estimate=pl.CostEstimate(flops=4 << 30, bytes_accessed=8 << 20, transcendentals=0),
    )(me, *operands)


def shift(x, step, n_rep):
    return lax.ppermute(x, "rep", [(i, (i + step) % n_rep) for i in range(n_rep)])


def ring_shift(x, step, n_table):
    return lax.ppermute(x, "table", [(i, (i + step * GROUP) % n_table) for i in range(n_table)])


def near_swap(x, other, n_table):
    return lax.ppermute(x, "table", [(i, i ^ other) for i in range(n_table)])


def near_exchange(same, other, n_table):
    swapped = near_swap(other, 1, n_table)
    got = [same, swapped]
    size = same.shape[0] // (GROUP // 2)
    for y in range(1, GROUP // 2):
        at = slice(y * size, (y + 1) * size)
        got.append(near_swap(jnp.concatenate([same[at], swapped[at]]), 2 * y, n_table))
    return got


def sum_kernel(own_ref, *refs):
    got, out_ref = refs[:-1], refs[-1]
    total = own_ref[...]
    for part in got:
        total = total + unpacked_across(part[...])
    if out_ref.dtype == I16:
        out_ref[...] = packed_across(total)
    else:
        half = total.shape[0] // 2
        pad = jnp.zeros((HALF - half, total.shape[1]), F32)
        out_ref[...] = jnp.concatenate([total[:half], pad, total[half:], pad], axis=0).T


def sum_call(own, got, shape, dtype):
    return pl.pallas_call(
        sum_kernel,
        in_specs=[vmem()] * (1 + len(got)),
        out_specs=vmem(),
        out_shape=jax.ShapeDtypeStruct(shape, dtype),
    )(own, *got)


def update_kernel(me_ref, table_ref, state_ref, *refs):
    parts, table_out, state_out = refs[:-2], refs[-2], refs[-1]
    n_rep = len(parts)
    width = table_ref.shape[0]
    for k in range(n_rep):
        quarter = parts[k].shape[1]
        q = lax.rem(me_ref[0] - k + n_rep, n_rep)
        at = pl.ds(pl.multiple_of(q * quarter, quarter), quarter)
        grad = unpacked_across(parts[k][...])
        state = state_ref[:, at] + jnp.sum(grad * grad, axis=0, keepdims=True) / width
        state_out[:, at] = state
        table_out[:, at] = table_ref[:, at] - learn_rate * grad / jnp.sqrt(state)


def cold_update(me, table, state, parts):
    rows, width = table.shape
    new_table, new_state = pl.pallas_call(
        update_kernel,
        in_specs=[smem()] + [vmem()] * (2 + len(parts)),
        out_specs=[vmem()] * 2,
        out_shape=[
            jax.ShapeDtypeStruct((width, rows), F32),
            jax.ShapeDtypeStruct((1, rows), F32),
        ],
        name="update",
    )(me, table.T, state[None, :], *parts)
    return new_table.T, new_state[0]


def pick_kernel(ids_ref, table_ref, out_ref):
    rows = table_ref.shape[0]
    slots = out_ref.shape[0]
    step = 512

    @pl.loop(0, slots // step)
    def _(c):
        at = pl.ds(pl.multiple_of(c * step, step), step)
        out_ref[at, :] = dot(mask_of((rows, step), ids_ref[:, at]), table_ref[...], TN).astype(BF)


def pick_call(ids, table):
    slots = ids.shape[1]
    return pl.pallas_call(
        pick_kernel,
        in_specs=[vmem()] * 2,
        out_specs=vmem(),
        out_shape=jax.ShapeDtypeStruct((slots, FULL), BF),
        cost_estimate=pl.CostEstimate(flops=2 << 30, bytes_accessed=3 << 20, transcendentals=0),
        name="pick",
    )(ids, table)


def adagrad(weights, state, grad):
    new_state = state + jnp.mean(grad * grad, axis=1)
    return (weights - learn_rate * grad / jnp.sqrt(new_state)[:, None], new_state)


def per_device(
    cold_table,
    cold_state,
    hot_table,
    hot_state,
    relations,
    head_owner,
    head_row,
    edge_rel,
    edge_tail,
    neg_ids,
):
    n_table = lax.axis_size("table")
    n_rep = lax.axis_size("rep")
    n_ring = n_table // GROUP
    edges = head_row.shape[0]
    width = cold_table.shape[1]
    cold_rows = cold_table.shape[0]
    hot_rows = hot_table.shape[0]
    negs = neg_ids.shape[1]
    near = [[z * GROUP + g for g in range(GROUP)] for z in range(n_ring)]
    far = [[z * GROUP + g for z in range(n_ring)] for g in range(GROUP)]

    per = HEAD_CAP + negs
    me = lax.axis_index("rep").astype(I32).reshape(1)

    place = lax.axis_index("table").astype(I32)
    ring_me, near_me = (place // GROUP).reshape(1), place % GROUP

    hot_bf = widen(hot_table.astype(BF))
    before_us = ring_shift(hot_bf, 1, n_table)
    after_us = ring_shift(hot_bf, n_ring - 1, n_table)
    here = jnp.concatenate([before_us, hot_bf, after_us])
    behind = ring_shift(here, 3, n_table)
    ahead = ring_shift(here, n_ring - 3, n_table)
    cold_bf = widen(cold_table.astype(BF))

    owner_hot = one_hot(head_owner[:, 0], n_table)
    row = lax.broadcasted_iota(jnp.int32, (edges, edges), 0)
    col = lax.broadcasted_iota(jnp.int32, (edges, edges), 1)
    before = dot((col < row).astype(BF), owner_hot, ((1,), (0,)))
    rank = jnp.sum(before * owner_hot.astype(F32), axis=1).astype(jnp.int32)
    head_slot = head_owner[:, 0] * per + rank

    edge_tail, _ = lax.optimization_barrier((edge_tail, here))
    block = edge_tail // hot_rows
    within = edge_tail % hot_rows
    block_hot = one_hot(block, n_table)
    within_hot = one_hot(within, hot_rows)
    present = (dot(block_hot, within_hot, ((0,), (0,))) > 0.5).astype(BF)
    prow = lax.broadcasted_iota(jnp.int32, (hot_rows, hot_rows), 0)
    pcol = lax.broadcasted_iota(jnp.int32, (hot_rows, hot_rows), 1)
    ranks = dot(present, (prow < pcol).astype(BF), ((1,), (0,)))
    rank_of = dot(block_hot, ranks.astype(BF), ((1,), (0,)))
    tail_rank = jnp.sum(rank_of * within_hot.astype(F32), axis=1).astype(jnp.int32)
    z_of, g_of = block // GROUP, block % GROUP
    tail_slot = ((g_of ^ near_me) * n_ring + z_of) * TAIL_CAP + tail_rank
    slot_iota = lax.broadcasted_iota(jnp.int32, (n_table, hot_rows, TAIL_CAP), 2)
    match = (ranks.astype(jnp.int32)[:, :, None] == slot_iota) & (present > 0.5)[:, :, None]
    row_iota = lax.broadcasted_iota(jnp.int32, (n_table, hot_rows, TAIL_CAP), 1) + 1
    slot_rows = jnp.sum(jnp.where(match, row_iota, 0), axis=1) - 1
    slot_rows = slot_rows.reshape(n_ring, GROUP, TAIL_CAP).transpose(1, 0, 2)

    wanted = jnp.zeros((n_table * per,), I32).at[head_slot].set(head_row).reshape(n_table, per)
    wanted = lax.all_to_all(wanted[:, :HEAD_CAP], "table", 0, 0)
    dense_rows = lax.all_to_all(
        slot_rows.reshape(GROUP, n_ring * TAIL_CAP), "table", 0, 0, axis_index_groups=near
    )
    dense_ids = dense_rows.reshape(GROUP, n_ring, TAIL_CAP)[jnp.arange(GROUP) ^ near_me]
    dense_ids = dense_ids.transpose(1, 0, 2).reshape(n_ring, GROUP * TAIL_CAP)
    own_negs = jnp.broadcast_to(neg_ids[0][None, :], (n_table, negs))
    asked = jnp.concatenate([wanted, own_negs], axis=1)
    head_ids = jnp.concatenate([wanted, jnp.full((n_table, negs), -1, I32)], axis=1)
    picked = pick_call(asked.reshape(1, n_table * per), cold_bf)
    rows = lax.all_to_all(picked.reshape(n_table, per, FULL), "table", 0, 0)
    relation = widen(relations[edge_rel])
    found = answer_call(ring_me, dense_ids, (here, behind, ahead))
    pieces = near_exchange(*found, n_table)
    same_msg, other_msg, back_msg = edge_call(
        head_slot, tail_slot, relation, rows.reshape(n_table * per, FULL), pieces
    )

    back = lax.all_to_all(back_msg.reshape(n_table, per, FULL), "table", 0, 0)
    tail_got = near_exchange(same_msg, other_msg, n_table)

    quarter = hot_rows // n_rep
    hot_own, *hot_msg = parts_call(
        dense_kernel,
        me,
        (dense_ids, *tail_got),
        width,
        n_ring * quarter,
        pltpu.VMEM((n_ring, hot_rows, FULL), F32),
        n_rep,
    )
    hot_got = [shift(hot_msg[k - 1], k, n_rep) for k in range(1, n_rep)]
    cold_own, *cold_msg = parts_call(
        cold_kernel,
        me,
        (head_ids.reshape(1, n_table * per), neg_ids, back),
        width,
        cold_rows // n_rep,
        pltpu.VMEM((n_table * per, FULL), BF),
        n_rep,
    )
    cold_got = []
    for k in range(1, n_rep):
        cold_got.append(shift(cold_msg[k - 1], k, n_rep))
    hot_own, _ = lax.optimization_barrier((hot_own, cold_own))
    hot_part = sum_call(hot_own, hot_got, (n_ring * quarter, FULL), F32)
    hot_rows_got = lax.all_to_all(
        hot_part.reshape(n_ring, quarter, FULL), "table", 0, 0, axis_index_groups=far
    )
    cold_part = sum_call(cold_own, cold_got, cold_got[0].shape, I16)
    cold_parts = [cold_part] + [shift(cold_part, k, n_rep) for k in range(1, n_rep)]
    hot_sum = jnp.sum(hot_rows_got, axis=0)
    new_cold_table, new_cold_state = cold_update(me, cold_table, cold_state, cold_parts)

    hot_parts = [hot_sum]
    for k in range(1, n_rep):
        hot_parts.append(shift(hot_sum, k, n_rep))
    hot_total = jnp.zeros((n_rep, quarter, FULL), F32)
    for k, part in enumerate(hot_parts):
        hot_total = lax.dynamic_update_index_in_dim(
            hot_total, part, lax.rem(me[0] - k + n_rep, n_rep), 0
        )
    hot_total = narrow(hot_total.reshape(hot_rows, FULL), width)
    new_hot_table, new_hot_state = adagrad(hot_table, hot_state, hot_total)
    return (new_cold_table, new_cold_state, new_hot_table, new_hot_state)


def solution(mesh):
    in_specs = (
        P("table", None),
        P("table"),
        P("table", None),
        P("table"),
        P(),
        P(("rep", "table"), None),
        P(("rep", "table")),
        P(("rep", "table")),
        P(("rep", "table")),
        P("rep", "table"),
    )
    out_specs = (P("table", None), P("table"), P("table", None), P("table"))

    return jax.shard_map(
        per_device, mesh=mesh, in_specs=in_specs, out_specs=out_specs, check_vma=False
    )
```

```python
import functools
import jax
import jax.numpy as jnp
from jax import lax
from jax.experimental import pallas as pl
from jax.experimental.pallas import tpu as pltpu
from jax.sharding import PartitionSpec as P


learn_rate = 0.5
HEAD_CAP = 16
TAIL_CAP = 32
GROUP = 8
HALF = 256
FULL = 2 * HALF

BF = jnp.bfloat16
I16 = jnp.int16
F32 = jnp.float32
I32 = jnp.int32


def dot(a, b, dims):
    return lax.dot_general(a, b, (dims, ((), ())), preferred_element_type=F32)


MM = ((1,), (0,))
NT = ((1,), (1,))
TN = ((0,), (0,))


def one_hot(ids, count):
    return (ids[:, None] == lax.broadcasted_iota(I32, (1, count), 1)).astype(BF)


def widen(rows):
    half = rows.shape[-1] // 2
    pad = [(0, 0)] * (rows.ndim - 1) + [(0, HALF - half)]
    return jnp.concatenate([jnp.pad(rows[..., :half], pad), jnp.pad(rows[..., half:], pad)], -1)


def narrow(rows, width):
    half = width // 2
    return jnp.concatenate([rows[..., :half], rows[..., HALF : HALF + half]], -1)


def mask_of(shape, ids_row, base=0):
    return (lax.broadcasted_iota(I32, shape, 0) + base == ids_row).astype(BF)


def two_part_dot(mask, x, dims=MM):
    hi = x.astype(BF)
    lo = (x - hi.astype(F32)).astype(BF)
    return dot(mask, hi, dims) + dot(mask, lo, dims)


def packed(x):
    peak = jnp.max(jnp.abs(x), axis=-1, keepdims=True)
    power = jnp.floor(jnp.log(jnp.maximum(peak, 1e-30)) * 1.4426950408889634)
    code = jnp.round(x * jnp.exp2(14.0 - power))
    lane = lax.broadcasted_iota(I32, x.shape, x.ndim - 1)
    code = jnp.where(lane >= FULL - 8, power, jnp.clip(code, -32767.0, 32767.0))
    return code.astype(I32).astype(I16)


def unpacked(code):
    x = code.astype(F32)
    lane = lax.broadcasted_iota(I32, x.shape, x.ndim - 1)
    scale = jnp.exp2(x[..., FULL - 1 :] - 14.0)
    return jnp.where(lane >= FULL - 8, 0.0, x * scale)


POWER_ROWS = 16


def across(x, width):
    half = width // 2
    x = x.T
    return jnp.concatenate([x[:half], x[HALF : HALF + half]], axis=0)


def packed_across(x):
    peak = jnp.max(jnp.abs(x), axis=0, keepdims=True)
    power = jnp.floor(jnp.log(jnp.maximum(peak, 1e-30)) * 1.4426950408889634)
    code = jnp.clip(jnp.round(x * jnp.exp2(14.0 - power)), -32767.0, 32767.0)
    power = jnp.broadcast_to(power, (POWER_ROWS, x.shape[1]))
    return jnp.concatenate([code, power], axis=0).astype(I32).astype(I16)


def unpacked_across(code):
    x = code.astype(F32)
    width = x.shape[0] - POWER_ROWS
    return x[:width] * jnp.exp2(x[width : width + 1] - 14.0)


def with_rel(rel, v):
    v_re, v_im, r_re, r_im = v[:, :HALF], v[:, HALF:], rel[:, :HALF], rel[:, HALF:]
    return jnp.concatenate([v_re * r_re - v_im * r_im, v_re * r_im + v_im * r_re], axis=1)


def against_rel(rel, v):
    v_re, v_im, r_re, r_im = v[:, :HALF], v[:, HALF:], rel[:, :HALF], rel[:, HALF:]
    return jnp.concatenate([r_re * v_re + r_im * v_im, r_re * v_im - r_im * v_re], axis=1)


def put(ref, value):
    ref[...] = value


def edge_kernel(slot_col, slot_row, tail_col, tail_row, rel_ref, rows_ref, *refs):
    pieces, (same_msg, other_msg, back_msg) = refs[:5], refs[5:8]
    found, heads, negs, hi_buf, lo_buf, head_buf, neg_buf = refs[8:]
    edges = slot_col.shape[0]
    owners, per, _ = rows_ref.shape
    slots = heads.shape[0]
    part = found.shape[0] // GROUP
    n_neg = negs.shape[0]
    found[:part, :] = pieces[0][:part, :]
    found[part : 2 * part, :] = pieces[1][:part, :]
    for y in range(1, GROUP // 2):
        found[2 * y * part : 2 * (y + 1) * part, :] = pieces[y + 1][...]
    halves = 2
    e_half, o_half = edges // halves, owners // halves
    s_half, n_half = slots // halves, n_neg // halves

    @pl.loop(0, halves)
    def _(c):
        rows = rows_ref[pl.ds(pl.multiple_of(c * o_half, o_half), o_half)].astype(F32)
        to = pl.ds(pl.multiple_of(c * s_half, s_half), s_half)
        heads[to, :] = rows[:, :HEAD_CAP, :].reshape(s_half, FULL).astype(BF)
        to = pl.ds(pl.multiple_of(c * n_half, n_half), n_half)
        negs[to, :] = rows[:, HEAD_CAP:, :].reshape(n_half, FULL).astype(BF)

    neg_buf[...] = jnp.zeros_like(neg_buf)

    @pl.loop(0, halves)
    def _(h):
        at = pl.ds(pl.multiple_of(h * e_half, e_half), e_half)
        rel = rel_ref[at, :]
        pick = tail_col[at, :] == lax.broadcasted_iota(I32, (e_half, GROUP * part), 1)
        tail_f = dot(pick.astype(BF), found[...], MM)
        pick = slot_col[at, :] == lax.broadcasted_iota(I32, (e_half, slots), 1)
        head_f = dot(pick.astype(BF), heads[...], MM)
        negatives = negs[...]
        queries = with_rel(rel, head_f)
        probes = against_rel(rel, tail_f)
        positive = jnp.sum(queries * tail_f, axis=1, keepdims=True)
        query_b = queries.astype(BF)
        probe_b = probes.astype(BF)
        pos_weight = -jax.nn.sigmoid(-positive)
        tail_weight = jax.nn.sigmoid(dot(query_b, negatives, NT)).astype(BF)
        head_weight = jax.nn.sigmoid(dot(probe_b, negatives, NT)).astype(BF)
        tail_mix = dot(tail_weight, negatives, MM)
        head_mix = dot(head_weight, negatives, MM)
        head_buf[at, :] = against_rel(rel, pos_weight * tail_f + tail_mix).astype(BF)
        tail_grad = with_rel(rel, pos_weight * head_f + head_mix)
        grad_hi = tail_grad.astype(BF)
        hi_buf[at, :] = grad_hi
        lo_buf[at, :] = (tail_grad - grad_hi.astype(F32)).astype(BF)
        neg_buf[...] += dot(tail_weight, query_b, TN) + dot(head_weight, probe_b, TN)

    @pl.loop(0, GROUP)
    def _(k):
        mask = mask_of((part, edges), tail_row[...], k * part)
        code = packed(dot(mask, hi_buf[...], MM) + dot(mask, lo_buf[...], MM))
        at = pl.ds(pl.multiple_of((k >> 1) * part, part), part)
        pl.when((k & 1) == 0)(functools.partial(put, same_msg.at[at], code))
        pl.when((k & 1) == 1)(functools.partial(put, other_msg.at[at], code))

    @pl.loop(0, halves)
    def _(c):
        back = dot(mask_of((s_half, edges), slot_row[...], c * s_half), head_buf[...], MM)
        grads = neg_buf[pl.ds(pl.multiple_of(c * n_half, n_half), n_half), :]
        back = [back.reshape(o_half, HEAD_CAP, FULL), grads.reshape(o_half, per - HEAD_CAP, FULL)]
        to = pl.ds(pl.multiple_of(c * o_half, o_half), o_half)
        back_msg[to] = packed(jnp.concatenate(back, axis=1))


def edge_call(head_slot, tail_slot, rel, rows, pieces):
    edges = head_slot.shape[0]
    owners, per, _ = rows.shape
    part = pieces[1].shape[0] * 2 // GROUP
    n_neg = owners * (per - HEAD_CAP)
    outs = pl.pallas_call(
        edge_kernel,
        in_specs=[vmem()] * (6 + len(pieces)),
        out_specs=[vmem()] * 3,
        out_shape=[jax.ShapeDtypeStruct((GROUP // 2 * part, FULL), I16)] * 2
        + [jax.ShapeDtypeStruct((owners, per, FULL), I16)],
        scratch_shapes=[
            pltpu.VMEM((GROUP * part, FULL), BF),
            pltpu.VMEM((owners * HEAD_CAP, FULL), BF),
            pltpu.VMEM((n_neg, FULL), BF),
            pltpu.VMEM((edges, FULL), BF),
            pltpu.VMEM((edges, FULL), BF),
            pltpu.VMEM((edges, FULL), BF),
            pltpu.VMEM((n_neg, FULL), F32),
        ],
        cost_estimate=pl.CostEstimate(flops=9 << 30, bytes_accessed=16 << 20, transcendentals=1 << 20),
        name="edge",
    )(
        head_slot[:, None],
        head_slot[None, :],
        tail_slot[:, None],
        tail_slot[None, :],
        rel,
        rows,
        *pieces,
    )
    return outs


def answer_kernel(me_ref, ids_ref, here, behind, ahead, same_out, other_out):
    n_ring = ids_ref.shape[0]
    rows = here.shape[0] // 3
    places = ((here, 1), (here, 0), (behind, 2), (behind, 1), (behind, 0), (ahead, 1), (ahead, 0), (here, 2))
    for k, (ref, i) in enumerate(places):
        z = lax.rem(me_ref[0] - k + n_ring, n_ring)
        mask = mask_of((rows, GROUP * TAIL_CAP), ids_ref[pl.ds(z, 1), :])
        found = dot(mask, ref[i * rows : (i + 1) * rows, :], TN).astype(BF)
        for g in range(GROUP):
            start = pl.multiple_of((g // 2) * n_ring * TAIL_CAP + z * TAIL_CAP, TAIL_CAP)
            out = other_out if g % 2 else same_out
            out[pl.ds(start, TAIL_CAP), :] = found[g * TAIL_CAP : (g + 1) * TAIL_CAP, :]


def answer_call(ring_me, ids, blocks):
    n_ring = ids.shape[0]
    out = jax.ShapeDtypeStruct((GROUP // 2 * n_ring * TAIL_CAP, FULL), BF)
    return pl.pallas_call(
        answer_kernel,
        in_specs=[smem()] + [vmem()] * (1 + len(blocks)),
        out_specs=[vmem()] * 2,
        out_shape=[out] * 2,
        cost_estimate=pl.CostEstimate(flops=1 << 30, bytes_accessed=4 << 20, transcendentals=0),
        name="answer",
    )(ring_me, ids, *blocks)


def coded_parts(src, own_ref, msgs, me, n_rep):
    @pl.loop(0, n_rep)
    def _(k):
        part = across(src(lax.rem(me + k, n_rep)), own_ref.shape[0])
        pl.when(k == 0)(functools.partial(put, own_ref, part))
        code = packed_across(part)
        for step in range(1, n_rep):
            pl.when(k == step)(functools.partial(put, msgs[step - 1], code))


def dense_kernel(me_ref, ids_ref, *refs, n_rep):
    got, own_ref, msgs, dense = refs[:5], refs[5], refs[6:-1], refs[-1]
    n_ring, rows, _ = dense.shape

    @pl.loop(0, n_ring)
    def _(z):
        at = pl.ds(pl.multiple_of(z * TAIL_CAP, TAIL_CAP), TAIL_CAP)
        then = pl.ds(pl.multiple_of((n_ring + z) * TAIL_CAP, TAIL_CAP), TAIL_CAP)
        part = [got[0][at, :], got[1][at, :]]
        for pair in got[2:]:
            part += [pair[at, :], pair[then, :]]
        part = [unpacked(code) for code in part]
        mask = mask_of((rows, GROUP * TAIL_CAP), ids_ref[pl.ds(z, 1), :])
        dense[z] = two_part_dot(mask, jnp.concatenate(part, axis=0))

    quarter = rows // n_rep

    def src(q):
        start = pl.multiple_of(q * quarter, quarter)
        return dense[:, pl.ds(start, quarter), :].reshape(n_ring * quarter, FULL)

    coded_parts(src, own_ref, msgs, me_ref[0], n_rep)


def cold_kernel(me_ref, ids_ref, neg_ref, back_ref, own_ref, *refs, n_rep):
    n_src, per, _ = back_ref.shape
    msgs, flat = refs[:-1], refs[-1]
    quarter = own_ref.shape[1]
    back = unpacked(back_ref[...])
    negs = per - HEAD_CAP
    neg_sum = jnp.sum(back[:, HEAD_CAP:, :], axis=0)
    flat[...] = back[:, :HEAD_CAP, :].reshape(n_src * HEAD_CAP, FULL).astype(BF)
    hi = neg_sum.astype(BF)
    rest = neg_sum - hi.astype(F32)

    def src(q):
        mask = mask_of((quarter, n_src * HEAD_CAP), ids_ref[...], q * quarter)
        neg_mask = mask_of((quarter, negs), neg_ref[...], q * quarter)
        return dot(mask, flat[...], MM) + dot(neg_mask, hi, MM) + two_part_dot(neg_mask, rest)

    coded_parts(src, own_ref, msgs, me_ref[0], n_rep)


def smem():
    return pl.BlockSpec(memory_space=pltpu.SMEM)


def vmem():
    return pl.BlockSpec(memory_space=pltpu.VMEM)


def parts_call(kernel, me, operands, width, rows, scratch, n_rep):
    return pl.pallas_call(
        functools.partial(kernel, n_rep=n_rep),
        in_specs=[smem()] + [vmem()] * len(operands),
        out_specs=[vmem()] * n_rep,
        out_shape=[jax.ShapeDtypeStruct((width, rows), F32)]
        + [jax.ShapeDtypeStruct((width + POWER_ROWS, rows), I16)] * (n_rep - 1),
        scratch_shapes=[scratch],
        cost_estimate=pl.CostEstimate(flops=4 << 30, bytes_accessed=8 << 20, transcendentals=0),
    )(me, *operands)


def shift(x, step, n_rep):
    return lax.ppermute(x, "rep", [(i, (i + step) % n_rep) for i in range(n_rep)])


def ring_shift(x, step, n_table):
    return lax.ppermute(x, "table", [(i, (i + step * GROUP) % n_table) for i in range(n_table)])


def near_swap(x, other, n_table):
    return lax.ppermute(x, "table", [(i, i ^ other) for i in range(n_table)])


def near_exchange(same, other, n_table):
    swapped = near_swap(other, 1, n_table)
    got = [same, swapped]
    size = same.shape[0] // (GROUP // 2)
    for y in range(1, GROUP // 2):
        at = slice(y * size, (y + 1) * size)
        got.append(near_swap(jnp.concatenate([same[at], swapped[at]]), 2 * y, n_table))
    return got


def sum_kernel(own_ref, *refs):
    got, out_ref = refs[:-1], refs[-1]
    total = own_ref[...]
    for part in got:
        total = total + unpacked_across(part[...])
    if out_ref.dtype == I16:
        out_ref[...] = packed_across(total)
    else:
        half = total.shape[0] // 2
        pad = jnp.zeros((HALF - half, total.shape[1]), F32)
        out_ref[...] = jnp.concatenate([total[:half], pad, total[half:], pad], axis=0).T


def sum_call(own, got, shape, dtype):
    return pl.pallas_call(
        sum_kernel,
        in_specs=[vmem()] * (1 + len(got)),
        out_specs=vmem(),
        out_shape=jax.ShapeDtypeStruct(shape, dtype),
    )(own, *got)


def update_kernel(me_ref, table_ref, state_ref, *refs):
    parts, table_out, state_out = refs[:-2], refs[-2], refs[-1]
    n_rep = len(parts)
    width = table_ref.shape[0]
    for k in range(n_rep):
        quarter = parts[k].shape[1]
        q = lax.rem(me_ref[0] - k + n_rep, n_rep)
        at = pl.ds(pl.multiple_of(q * quarter, quarter), quarter)
        grad = unpacked_across(parts[k][...])
        state = state_ref[:, at] + jnp.sum(grad * grad, axis=0, keepdims=True) / width
        state_out[:, at] = state
        table_out[:, at] = table_ref[:, at] - learn_rate * grad / jnp.sqrt(state)


def cold_update(me, table, state, parts):
    rows, width = table.shape
    new_table, new_state = pl.pallas_call(
        update_kernel,
        in_specs=[smem()] + [vmem()] * (2 + len(parts)),
        out_specs=[vmem()] * 2,
        out_shape=[
            jax.ShapeDtypeStruct((width, rows), F32),
            jax.ShapeDtypeStruct((1, rows), F32),
        ],
        name="update",
    )(me, table.T, state[None, :], *parts)
    return new_table.T, new_state[0]


def pick_kernel(ids_ref, neg_ref, table_ref, out_ref):
    rows = table_ref.shape[0]
    negs = neg_ref.shape[0]
    dests = 32
    step = dests * HEAD_CAP
    mask = (neg_ref[...] == lax.broadcasted_iota(I32, (negs, rows), 1)).astype(BF)
    neg_rows = jnp.broadcast_to(dot(mask, table_ref[...], MM)[None], (dests, negs, FULL))

    @pl.loop(0, out_ref.shape[0] // dests)
    def _(c):
        at = pl.ds(pl.multiple_of(c * step, step), step)
        mask = (ids_ref[at, :] == lax.broadcasted_iota(I32, (step, rows), 1)).astype(BF)
        found = dot(mask, table_ref[...], MM).reshape(dests, HEAD_CAP, FULL)
        to = pl.ds(pl.multiple_of(c * dests, dests), dests)
        out_ref[to] = jnp.concatenate([found, neg_rows], axis=1).astype(BF)


def pick_call(ids, neg_ids, table):
    dests = ids.shape[0] // HEAD_CAP
    return pl.pallas_call(
        pick_kernel,
        in_specs=[vmem()] * 3,
        out_specs=vmem(),
        out_shape=jax.ShapeDtypeStruct((dests, HEAD_CAP + neg_ids.shape[0], FULL), BF),
        cost_estimate=pl.CostEstimate(flops=2 << 30, bytes_accessed=3 << 20, transcendentals=0),
        name="pick",
    )(ids, neg_ids, table)


def adagrad(weights, state, grad):
    new_state = state + jnp.mean(grad * grad, axis=1)
    return (weights - learn_rate * grad / jnp.sqrt(new_state)[:, None], new_state)


def per_device(
    cold_table,
    cold_state,
    hot_table,
    hot_state,
    relations,
    head_owner,
    head_row,
    edge_rel,
    edge_tail,
    neg_ids,
):
    n_table = lax.axis_size("table")
    n_rep = lax.axis_size("rep")
    n_ring = n_table // GROUP
    edges = head_row.shape[0]
    width = cold_table.shape[1]
    cold_rows = cold_table.shape[0]
    hot_rows = hot_table.shape[0]
    near = [[z * GROUP + g for g in range(GROUP)] for z in range(n_ring)]
    far = [[z * GROUP + g for z in range(n_ring)] for g in range(GROUP)]

    me = lax.axis_index("rep").astype(I32).reshape(1)

    place = lax.axis_index("table").astype(I32)
    ring_me, near_me = (place // GROUP).reshape(1), place % GROUP

    hot_bf = widen(hot_table.astype(BF))
    before_us = ring_shift(hot_bf, 1, n_table)
    after_us = ring_shift(hot_bf, n_ring - 1, n_table)
    here = jnp.concatenate([before_us, hot_bf, after_us])
    behind = ring_shift(here, 3, n_table)
    ahead = ring_shift(here, n_ring - 3, n_table)
    cold_bf = widen(cold_table.astype(BF))

    owner_hot = one_hot(head_owner[:, 0], n_table)
    row = lax.broadcasted_iota(jnp.int32, (edges, edges), 0)
    col = lax.broadcasted_iota(jnp.int32, (edges, edges), 1)
    before = dot((col < row).astype(BF), owner_hot, ((1,), (0,)))
    rank = jnp.sum(before * owner_hot.astype(F32), axis=1).astype(jnp.int32)
    head_slot = head_owner[:, 0] * HEAD_CAP + rank

    edge_tail, _ = lax.optimization_barrier((edge_tail, here))
    block = edge_tail // hot_rows
    within = edge_tail % hot_rows
    block_hot = one_hot(block, n_table)
    within_hot = one_hot(within, hot_rows)
    present = (dot(block_hot, within_hot, ((0,), (0,))) > 0.5).astype(BF)
    prow = lax.broadcasted_iota(jnp.int32, (hot_rows, hot_rows), 0)
    pcol = lax.broadcasted_iota(jnp.int32, (hot_rows, hot_rows), 1)
    ranks = dot(present, (prow < pcol).astype(BF), ((1,), (0,)))
    rank_of = dot(block_hot, ranks.astype(BF), ((1,), (0,)))
    tail_rank = jnp.sum(rank_of * within_hot.astype(F32), axis=1).astype(jnp.int32)
    z_of, g_of = block // GROUP, block % GROUP
    tail_slot = ((g_of ^ near_me) * n_ring + z_of) * TAIL_CAP + tail_rank
    slot_iota = lax.broadcasted_iota(jnp.int32, (n_table, hot_rows, TAIL_CAP), 2)
    match = (ranks.astype(jnp.int32)[:, :, None] == slot_iota) & (present > 0.5)[:, :, None]
    row_iota = lax.broadcasted_iota(jnp.int32, (n_table, hot_rows, TAIL_CAP), 1) + 1
    slot_rows = jnp.sum(jnp.where(match, row_iota, 0), axis=1) - 1
    slot_rows = slot_rows.reshape(n_ring, GROUP, TAIL_CAP).transpose(1, 0, 2)

    wanted = jnp.zeros((n_table * HEAD_CAP,), I32).at[head_slot].set(head_row)
    wanted = wanted.reshape(n_table, HEAD_CAP)
    wanted = lax.all_to_all(wanted, "table", 0, 0)
    dense_rows = lax.all_to_all(
        slot_rows.reshape(GROUP, n_ring * TAIL_CAP), "table", 0, 0, axis_index_groups=near
    )
    dense_ids = dense_rows.reshape(GROUP, n_ring, TAIL_CAP)[jnp.arange(GROUP) ^ near_me]
    dense_ids = dense_ids.transpose(1, 0, 2).reshape(n_ring, GROUP * TAIL_CAP)
    picked = pick_call(wanted.reshape(n_table * HEAD_CAP, 1), neg_ids.T, cold_bf)
    rows = lax.all_to_all(picked, "table", 0, 0)
    relation = widen(relations[edge_rel])
    found = answer_call(ring_me, dense_ids, (here, behind, ahead))
    pieces = near_exchange(*found, n_table)
    same_msg, other_msg, back_msg = edge_call(
        head_slot, tail_slot, relation, rows, pieces
    )

    back = lax.all_to_all(back_msg, "table", 0, 0)
    tail_got = near_exchange(same_msg, other_msg, n_table)

    quarter = hot_rows // n_rep
    hot_own, *hot_msg = parts_call(
        dense_kernel,
        me,
        (dense_ids, *tail_got),
        width,
        n_ring * quarter,
        pltpu.VMEM((n_ring, hot_rows, FULL), F32),
        n_rep,
    )
    hot_got = [shift(hot_msg[k - 1], k, n_rep) for k in range(1, n_rep)]
    cold_own, *cold_msg = parts_call(
        cold_kernel,
        me,
        (wanted.reshape(1, n_table * HEAD_CAP), neg_ids, back),
        width,
        cold_rows // n_rep,
        pltpu.VMEM((n_table * HEAD_CAP, FULL), BF),
        n_rep,
    )
    cold_got = []
    for k in range(1, n_rep):
        cold_got.append(shift(cold_msg[k - 1], k, n_rep))
    hot_own, _ = lax.optimization_barrier((hot_own, cold_own))
    hot_part = sum_call(hot_own, hot_got, (n_ring * quarter, FULL), F32)
    hot_rows_got = lax.all_to_all(
        hot_part.reshape(n_ring, quarter, FULL), "table", 0, 0, axis_index_groups=far
    )
    cold_part = sum_call(cold_own, cold_got, cold_got[0].shape, I16)
    cold_parts = [cold_part] + [shift(cold_part, k, n_rep) for k in range(1, n_rep)]
    hot_sum = jnp.sum(hot_rows_got, axis=0)
    new_cold_table, new_cold_state = cold_update(me, cold_table, cold_state, cold_parts)

    hot_parts = [hot_sum]
    for k in range(1, n_rep):
        hot_parts.append(shift(hot_sum, k, n_rep))
    hot_total = jnp.zeros((n_rep, quarter, FULL), F32)
    for k, part in enumerate(hot_parts):
        hot_total = lax.dynamic_update_index_in_dim(
            hot_total, part, lax.rem(me[0] - k + n_rep, n_rep), 0
        )
    hot_total = narrow(hot_total.reshape(hot_rows, FULL), width)
    new_hot_table, new_hot_state = adagrad(hot_table, hot_state, hot_total)
    return (new_cold_table, new_cold_state, new_hot_table, new_hot_state)


def solution(mesh):
    in_specs = (
        P("table", None),
        P("table"),
        P("table", None),
        P("table"),
        P(),
        P(("rep", "table"), None),
        P(("rep", "table")),
        P(("rep", "table")),
        P(("rep", "table")),
        P("rep", "table"),
    )
    out_specs = (P("table", None), P("table"), P("table", None), P("table"))

    return jax.shard_map(
        per_device, mesh=mesh, in_specs=in_specs, out_specs=out_specs, check_vma=False
    )
```

```python
import functools
import jax
import jax.numpy as jnp
from jax import lax
from jax.experimental import pallas as pl
from jax.experimental.pallas import tpu as pltpu
from jax.sharding import PartitionSpec as P


learn_rate = 0.5
HEAD_CAP = 16
TAIL_CAP = 32
GROUP = 8
HALF = 256
FULL = 2 * HALF

BF = jnp.bfloat16
I16 = jnp.int16
F32 = jnp.float32
I32 = jnp.int32


def dot(a, b, dims):
    return lax.dot_general(a, b, (dims, ((), ())), preferred_element_type=F32)


MM = ((1,), (0,))
NT = ((1,), (1,))
TN = ((0,), (0,))


def one_hot(ids, count):
    return (ids[:, None] == lax.broadcasted_iota(I32, (1, count), 1)).astype(BF)


def widen(rows):
    half = rows.shape[-1] // 2
    pad = [(0, 0)] * (rows.ndim - 1) + [(0, HALF - half)]
    return jnp.concatenate([jnp.pad(rows[..., :half], pad), jnp.pad(rows[..., half:], pad)], -1)


def narrow(rows, width):
    half = width // 2
    return jnp.concatenate([rows[..., :half], rows[..., HALF : HALF + half]], -1)


def mask_of(shape, ids_row, base=0):
    return (lax.broadcasted_iota(I32, shape, 0) + base == ids_row).astype(BF)


def two_part_dot(mask, x, dims=MM):
    hi = x.astype(BF)
    lo = (x - hi.astype(F32)).astype(BF)
    return dot(mask, hi, dims) + dot(mask, lo, dims)


def packed(x):
    peak = jnp.max(jnp.abs(x), axis=-1, keepdims=True)
    power = jnp.floor(jnp.log(jnp.maximum(peak, 1e-30)) * 1.4426950408889634)
    code = jnp.round(x * jnp.exp2(14.0 - power))
    lane = lax.broadcasted_iota(I32, x.shape, x.ndim - 1)
    code = jnp.where(lane >= FULL - 8, power, jnp.clip(code, -32767.0, 32767.0))
    return code.astype(I32).astype(I16)


def unpacked(code):
    x = code.astype(F32)
    lane = lax.broadcasted_iota(I32, x.shape, x.ndim - 1)
    scale = jnp.exp2(x[..., FULL - 1 :] - 14.0)
    return jnp.where(lane >= FULL - 8, 0.0, x * scale)


POWER_ROWS = 16


def across(x, width):
    half = width // 2
    x = x.T
    return jnp.concatenate([x[:half], x[HALF : HALF + half]], axis=0)


def packed_across(x):
    peak = jnp.max(jnp.abs(x), axis=0, keepdims=True)
    power = jnp.floor(jnp.log(jnp.maximum(peak, 1e-30)) * 1.4426950408889634)
    code = jnp.clip(jnp.round(x * jnp.exp2(14.0 - power)), -32767.0, 32767.0)
    power = jnp.broadcast_to(power, (POWER_ROWS, x.shape[1]))
    return jnp.concatenate([code, power], axis=0).astype(I32).astype(I16)


def unpacked_across(code):
    x = code.astype(F32)
    width = x.shape[0] - POWER_ROWS
    return x[:width] * jnp.exp2(x[width : width + 1] - 14.0)


def with_rel(rel, v):
    v_re, v_im, r_re, r_im = v[:, :HALF], v[:, HALF:], rel[:, :HALF], rel[:, HALF:]
    return jnp.concatenate([v_re * r_re - v_im * r_im, v_re * r_im + v_im * r_re], axis=1)


def against_rel(rel, v):
    v_re, v_im, r_re, r_im = v[:, :HALF], v[:, HALF:], rel[:, :HALF], rel[:, HALF:]
    return jnp.concatenate([r_re * v_re + r_im * v_im, r_re * v_im - r_im * v_re], axis=1)


def put(ref, value):
    ref[...] = value


def edge_kernel(slot_col, slot_row, tail_col, tail_row, rel_ref, rows_ref, *refs):
    pieces, (same_msg, other_msg, back_msg) = refs[:5], refs[5:8]
    found, heads, negs, hi_buf, lo_buf, head_buf, neg_buf = refs[8:]
    edges = slot_col.shape[0]
    owners, per, _ = rows_ref.shape
    slots = heads.shape[0]
    part = found.shape[0] // GROUP
    n_neg = negs.shape[0]
    found[:part, :] = pieces[0][:part, :]
    found[part : 2 * part, :] = pieces[1][:part, :]
    for y in range(1, GROUP // 2):
        found[2 * y * part : 2 * (y + 1) * part, :] = pieces[y + 1][...]
    halves = 2
    e_half, o_half = edges // halves, owners // halves
    s_half, n_half = slots // halves, n_neg // halves

    @pl.loop(0, halves)
    def _(c):
        rows = rows_ref[pl.ds(pl.multiple_of(c * o_half, o_half), o_half)].astype(F32)
        to = pl.ds(pl.multiple_of(c * s_half, s_half), s_half)
        heads[to, :] = rows[:, :HEAD_CAP, :].reshape(s_half, FULL).astype(BF)
        to = pl.ds(pl.multiple_of(c * n_half, n_half), n_half)
        negs[to, :] = rows[:, HEAD_CAP:, :].reshape(n_half, FULL).astype(BF)

    neg_buf[...] = jnp.zeros_like(neg_buf)

    @pl.loop(0, halves)
    def _(h):
        at = pl.ds(pl.multiple_of(h * e_half, e_half), e_half)
        rel = rel_ref[at, :]
        pick = tail_col[at, :] == lax.broadcasted_iota(I32, (e_half, GROUP * part), 1)
        tail_f = dot(pick.astype(BF), found[...], MM)
        pick = slot_col[at, :] == lax.broadcasted_iota(I32, (e_half, slots), 1)
        head_f = dot(pick.astype(BF), heads[...], MM)
        negatives = negs[...]
        queries = with_rel(rel, head_f)
        probes = against_rel(rel, tail_f)
        positive = jnp.sum(queries * tail_f, axis=1, keepdims=True)
        query_b = queries.astype(BF)
        probe_b = probes.astype(BF)
        pos_weight = -jax.nn.sigmoid(-positive)
        tail_weight = jax.nn.sigmoid(dot(query_b, negatives, NT)).astype(BF)
        head_weight = jax.nn.sigmoid(dot(probe_b, negatives, NT)).astype(BF)
        tail_mix = dot(tail_weight, negatives, MM)
        head_mix = dot(head_weight, negatives, MM)
        head_buf[at, :] = against_rel(rel, pos_weight * tail_f + tail_mix).astype(BF)
        tail_grad = with_rel(rel, pos_weight * head_f + head_mix)
        grad_hi = tail_grad.astype(BF)
        hi_buf[at, :] = grad_hi
        lo_buf[at, :] = (tail_grad - grad_hi.astype(F32)).astype(BF)
        neg_buf[...] += dot(tail_weight, query_b, TN) + dot(head_weight, probe_b, TN)

    @pl.loop(0, GROUP)
    def _(k):
        mask = mask_of((part, edges), tail_row[...], k * part)
        code = packed(dot(mask, hi_buf[...], MM) + dot(mask, lo_buf[...], MM))
        at = pl.ds(pl.multiple_of((k >> 1) * part, part), part)
        pl.when((k & 1) == 0)(functools.partial(put, same_msg.at[at], code))
        pl.when((k & 1) == 1)(functools.partial(put, other_msg.at[at], code))

    @pl.loop(0, halves)
    def _(c):
        back = dot(mask_of((s_half, edges), slot_row[...], c * s_half), head_buf[...], MM)
        grads = neg_buf[pl.ds(pl.multiple_of(c * n_half, n_half), n_half), :]
        back = [back.reshape(o_half, HEAD_CAP, FULL), grads.reshape(o_half, per - HEAD_CAP, FULL)]
        to = pl.ds(pl.multiple_of(c * o_half, o_half), o_half)
        back_msg[to] = packed(jnp.concatenate(back, axis=1))


def edge_call(head_slot, tail_slot, rel, rows, pieces):
    edges = head_slot.shape[0]
    owners, per, _ = rows.shape
    part = pieces[1].shape[0] * 2 // GROUP
    n_neg = owners * (per - HEAD_CAP)
    outs = pl.pallas_call(
        edge_kernel,
        in_specs=[vmem()] * (6 + len(pieces)),
        out_specs=[vmem()] * 3,
        out_shape=[jax.ShapeDtypeStruct((GROUP // 2 * part, FULL), I16)] * 2
        + [jax.ShapeDtypeStruct((owners, per, FULL), I16)],
        scratch_shapes=[
            pltpu.VMEM((GROUP * part, FULL), BF),
            pltpu.VMEM((owners * HEAD_CAP, FULL), BF),
            pltpu.VMEM((n_neg, FULL), BF),
            pltpu.VMEM((edges, FULL), BF),
            pltpu.VMEM((edges, FULL), BF),
            pltpu.VMEM((edges, FULL), BF),
            pltpu.VMEM((n_neg, FULL), F32),
        ],
        cost_estimate=pl.CostEstimate(flops=9 << 30, bytes_accessed=16 << 20, transcendentals=1 << 20),
        name="edge",
    )(
        head_slot[:, None],
        head_slot[None, :],
        tail_slot[:, None],
        tail_slot[None, :],
        rel,
        rows,
        *pieces,
    )
    return outs


def answer_kernel(me_ref, ids_ref, here, behind, ahead, same_out, other_out):
    n_ring = ids_ref.shape[0]
    rows = here.shape[0] // 3
    places = ((here, 1), (here, 0), (behind, 2), (behind, 1), (behind, 0), (ahead, 1), (ahead, 0), (here, 2))
    for k, (ref, i) in enumerate(places):
        z = lax.rem(me_ref[0] - k + n_ring, n_ring)
        mask = mask_of((rows, GROUP * TAIL_CAP), ids_ref[pl.ds(z, 1), :])
        found = dot(mask, ref[i * rows : (i + 1) * rows, :], TN).astype(BF)
        for g in range(GROUP):
            start = pl.multiple_of((g // 2) * n_ring * TAIL_CAP + z * TAIL_CAP, TAIL_CAP)
            out = other_out if g % 2 else same_out
            out[pl.ds(start, TAIL_CAP), :] = found[g * TAIL_CAP : (g + 1) * TAIL_CAP, :]


def answer_call(ring_me, ids, blocks):
    n_ring = ids.shape[0]
    out = jax.ShapeDtypeStruct((GROUP // 2 * n_ring * TAIL_CAP, FULL), BF)
    return pl.pallas_call(
        answer_kernel,
        in_specs=[smem()] + [vmem()] * (1 + len(blocks)),
        out_specs=[vmem()] * 2,
        out_shape=[out] * 2,
        cost_estimate=pl.CostEstimate(flops=1 << 30, bytes_accessed=4 << 20, transcendentals=0),
        name="answer",
    )(ring_me, ids, *blocks)


def coded_parts(src, own_ref, msgs, me, n_rep):
    @pl.loop(0, n_rep)
    def _(k):
        part = across(src(lax.rem(me + k, n_rep)), own_ref.shape[0])
        pl.when(k == 0)(functools.partial(put, own_ref, part))
        code = packed_across(part)
        for step in range(1, n_rep):
            pl.when(k == step)(functools.partial(put, msgs[step - 1], code))


def dense_kernel(me_ref, ids_ref, *refs, n_rep):
    got, own_ref, msgs, dense = refs[:5], refs[5], refs[6:-1], refs[-1]
    n_ring, rows, _ = dense.shape

    @pl.loop(0, n_ring)
    def _(z):
        at = pl.ds(pl.multiple_of(z * TAIL_CAP, TAIL_CAP), TAIL_CAP)
        then = pl.ds(pl.multiple_of((n_ring + z) * TAIL_CAP, TAIL_CAP), TAIL_CAP)
        part = [got[0][at, :], got[1][at, :]]
        for pair in got[2:]:
            part += [pair[at, :], pair[then, :]]
        part = [unpacked(code) for code in part]
        mask = mask_of((rows, GROUP * TAIL_CAP), ids_ref[pl.ds(z, 1), :])
        dense[z] = two_part_dot(mask, jnp.concatenate(part, axis=0))

    quarter = rows // n_rep

    def src(q):
        start = pl.multiple_of(q * quarter, quarter)
        return dense[:, pl.ds(start, quarter), :].reshape(n_ring * quarter, FULL)

    coded_parts(src, own_ref, msgs, me_ref[0], n_rep)


def cold_kernel(me_ref, ids_ref, neg_ref, back_ref, own_ref, *refs, n_rep):
    n_src, per, _ = back_ref.shape
    msgs, flat = refs[:-1], refs[-1]
    quarter = own_ref.shape[1]
    back = unpacked(back_ref[...])
    negs = per - HEAD_CAP
    neg_sum = jnp.sum(back[:, HEAD_CAP:, :], axis=0)
    flat[...] = back[:, :HEAD_CAP, :].reshape(n_src * HEAD_CAP, FULL).astype(BF)
    hi = neg_sum.astype(BF)
    rest = neg_sum - hi.astype(F32)

    def src(q):
        mask = mask_of((quarter, n_src * HEAD_CAP), ids_ref[...], q * quarter)
        neg_mask = mask_of((quarter, negs), neg_ref[...], q * quarter)
        return dot(mask, flat[...], MM) + dot(neg_mask, hi, MM) + two_part_dot(neg_mask, rest)

    coded_parts(src, own_ref, msgs, me_ref[0], n_rep)


def smem():
    return pl.BlockSpec(memory_space=pltpu.SMEM)


def vmem():
    return pl.BlockSpec(memory_space=pltpu.VMEM)


def parts_call(kernel, me, operands, width, rows, scratch, n_rep):
    return pl.pallas_call(
        functools.partial(kernel, n_rep=n_rep),
        in_specs=[smem()] + [vmem()] * len(operands),
        out_specs=[vmem()] * n_rep,
        out_shape=[jax.ShapeDtypeStruct((width, rows), F32)]
        + [jax.ShapeDtypeStruct((width + POWER_ROWS, rows), I16)] * (n_rep - 1),
        scratch_shapes=[scratch],
        cost_estimate=pl.CostEstimate(flops=4 << 30, bytes_accessed=8 << 20, transcendentals=0),
    )(me, *operands)


def shift(x, step, n_rep):
    return lax.ppermute(x, "rep", [(i, (i + step) % n_rep) for i in range(n_rep)])


def ring_shift(x, step, n_table):
    return lax.ppermute(x, "table", [(i, (i + step * GROUP) % n_table) for i in range(n_table)])


def near_swap(x, other, n_table):
    return lax.ppermute(x, "table", [(i, i ^ other) for i in range(n_table)])


def near_exchange(same, other, n_table):
    swapped = near_swap(other, 1, n_table)
    got = [same, swapped]
    size = same.shape[0] // (GROUP // 2)
    for y in range(1, GROUP // 2):
        at = slice(y * size, (y + 1) * size)
        got.append(near_swap(jnp.concatenate([same[at], swapped[at]]), 2 * y, n_table))
    return got


def sum_kernel(own_ref, *refs):
    got, out_ref = refs[:-1], refs[-1]
    total = own_ref[...]
    for part in got:
        total = total + unpacked_across(part[...])
    if out_ref.dtype == I16:
        out_ref[...] = packed_across(total)
    else:
        half = total.shape[0] // 2
        pad = jnp.zeros((HALF - half, total.shape[1]), F32)
        out_ref[...] = jnp.concatenate([total[:half], pad, total[half:], pad], axis=0).T


def sum_call(own, got, shape, dtype):
    return pl.pallas_call(
        sum_kernel,
        in_specs=[vmem()] * (1 + len(got)),
        out_specs=vmem(),
        out_shape=jax.ShapeDtypeStruct(shape, dtype),
    )(own, *got)


def update_kernel(me_ref, table_ref, state_ref, *refs):
    parts, table_out, state_out = refs[:-2], refs[-2], refs[-1]
    n_rep = len(parts)
    width = table_ref.shape[0]
    for k in range(n_rep):
        quarter = parts[k].shape[1]
        q = lax.rem(me_ref[0] - k + n_rep, n_rep)
        at = pl.ds(pl.multiple_of(q * quarter, quarter), quarter)
        grad = unpacked_across(parts[k][...])
        state = state_ref[:, at] + jnp.sum(grad * grad, axis=0, keepdims=True) / width
        state_out[:, at] = state
        table_out[:, at] = table_ref[:, at] - learn_rate * grad / jnp.sqrt(state)


def cold_update(me, table, state, parts):
    rows, width = table.shape
    new_table, new_state = pl.pallas_call(
        update_kernel,
        in_specs=[smem()] + [vmem()] * (2 + len(parts)),
        out_specs=[vmem()] * 2,
        out_shape=[
            jax.ShapeDtypeStruct((width, rows), F32),
            jax.ShapeDtypeStruct((1, rows), F32),
        ],
        name="update",
    )(me, table.T, state[None, :], *parts)
    return new_table.T, new_state[0]


def pick_kernel(ids_ref, neg_ref, table_ref, out_ref):
    rows = table_ref.shape[0]
    negs = neg_ref.shape[0]
    dests = 32
    step = dests * HEAD_CAP
    mask = (neg_ref[...] == lax.broadcasted_iota(I32, (negs, rows), 1)).astype(BF)
    neg_rows = jnp.broadcast_to(dot(mask, table_ref[...], MM)[None], (dests, negs, FULL))

    @pl.loop(0, out_ref.shape[0] // dests)
    def _(c):
        at = pl.ds(pl.multiple_of(c * step, step), step)
        mask = (ids_ref[at, :] == lax.broadcasted_iota(I32, (step, rows), 1)).astype(BF)
        found = dot(mask, table_ref[...], MM).reshape(dests, HEAD_CAP, FULL)
        to = pl.ds(pl.multiple_of(c * dests, dests), dests)
        out_ref[to] = jnp.concatenate([found, neg_rows], axis=1).astype(BF)


def pick_call(ids, neg_ids, table):
    dests = ids.shape[0] // HEAD_CAP
    return pl.pallas_call(
        pick_kernel,
        in_specs=[vmem()] * 3,
        out_specs=vmem(),
        out_shape=jax.ShapeDtypeStruct((dests, HEAD_CAP + neg_ids.shape[0], FULL), BF),
        cost_estimate=pl.CostEstimate(flops=2 << 30, bytes_accessed=3 << 20, transcendentals=0),
        name="pick",
    )(ids, neg_ids, table)


def adagrad(weights, state, grad):
    new_state = state + jnp.mean(grad * grad, axis=1)
    return (weights - learn_rate * grad / jnp.sqrt(new_state)[:, None], new_state)


def per_device(
    cold_table,
    cold_state,
    hot_table,
    hot_state,
    relations,
    head_owner,
    head_row,
    edge_rel,
    edge_tail,
    neg_ids,
):
    n_table = lax.axis_size("table")
    n_rep = lax.axis_size("rep")
    n_ring = n_table // GROUP
    edges = head_row.shape[0]
    width = cold_table.shape[1]
    cold_rows = cold_table.shape[0]
    hot_rows = hot_table.shape[0]
    near = [[z * GROUP + g for g in range(GROUP)] for z in range(n_ring)]
    far = [[z * GROUP + g for z in range(n_ring)] for g in range(GROUP)]

    me = lax.axis_index("rep").astype(I32).reshape(1)

    place = lax.axis_index("table").astype(I32)
    ring_me, near_me = (place // GROUP).reshape(1), place % GROUP

    hot_bf = widen(hot_table.astype(BF))
    before_us = ring_shift(hot_bf, 1, n_table)
    after_us = ring_shift(hot_bf, n_ring - 1, n_table)
    here = jnp.concatenate([before_us, hot_bf, after_us])
    behind = ring_shift(here, 3, n_table)
    ahead = ring_shift(here, n_ring - 3, n_table)
    cold_bf = widen(cold_table.astype(BF))

    owner_hot = one_hot(head_owner[:, 0], n_table)
    row = lax.broadcasted_iota(jnp.int32, (edges, edges), 0)
    col = lax.broadcasted_iota(jnp.int32, (edges, edges), 1)
    before = dot((col < row).astype(BF), owner_hot, ((1,), (0,)))
    rank = jnp.sum(before * owner_hot.astype(F32), axis=1).astype(jnp.int32)
    head_slot = head_owner[:, 0] * HEAD_CAP + rank

    edge_tail, _ = lax.optimization_barrier((edge_tail, here))
    block = edge_tail // hot_rows
    within = edge_tail % hot_rows
    block_hot = one_hot(block, n_table)
    within_hot = one_hot(within, hot_rows)
    present = (dot(block_hot, within_hot, ((0,), (0,))) > 0.5).astype(BF)
    prow = lax.broadcasted_iota(jnp.int32, (hot_rows, hot_rows), 0)
    pcol = lax.broadcasted_iota(jnp.int32, (hot_rows, hot_rows), 1)
    ranks = dot(present, (prow < pcol).astype(BF), ((1,), (0,)))
    rank_of = dot(block_hot, ranks.astype(BF), ((1,), (0,)))
    tail_rank = jnp.sum(rank_of * within_hot.astype(F32), axis=1).astype(jnp.int32)
    z_of, g_of = block // GROUP, block % GROUP
    tail_slot = ((g_of ^ near_me) * n_ring + z_of) * TAIL_CAP + tail_rank
    slot_iota = lax.broadcasted_iota(jnp.int32, (n_table, hot_rows, TAIL_CAP), 2)
    match = (ranks.astype(jnp.int32)[:, :, None] == slot_iota) & (present > 0.5)[:, :, None]
    row_iota = lax.broadcasted_iota(jnp.int32, (n_table, hot_rows, TAIL_CAP), 1) + 1
    slot_rows = jnp.sum(jnp.where(match, row_iota, 0), axis=1) - 1
    slot_rows = slot_rows.reshape(n_ring, GROUP, TAIL_CAP).transpose(1, 0, 2)

    wanted = jnp.zeros((n_table * HEAD_CAP,), I32).at[head_slot].set(head_row)
    wanted = wanted.reshape(n_table, HEAD_CAP)
    wanted = lax.all_to_all(wanted, "table", 0, 0)
    dense_rows = lax.all_to_all(
        slot_rows.reshape(GROUP, n_ring * TAIL_CAP), "table", 0, 0, axis_index_groups=near
    )
    dense_ids = dense_rows.reshape(GROUP, n_ring, TAIL_CAP)[jnp.arange(GROUP) ^ near_me]
    dense_ids = dense_ids.transpose(1, 0, 2).reshape(n_ring, GROUP * TAIL_CAP)
    picked = pick_call(wanted.reshape(n_table * HEAD_CAP, 1), neg_ids.T, cold_bf)
    rows = lax.all_to_all(picked, "table", 0, 0)
    relation = widen(relations[edge_rel])
    found = answer_call(ring_me, dense_ids, (here, behind, ahead))
    pieces = near_exchange(*found, n_table)
    same_msg, other_msg, back_msg = edge_call(
        head_slot, tail_slot, relation, rows, pieces
    )

    back = lax.all_to_all(back_msg, "table", 0, 0)
    tail_got = near_exchange(same_msg, other_msg, n_table)

    quarter = hot_rows // n_rep
    hot_own, *hot_msg = parts_call(
        dense_kernel,
        me,
        (dense_ids, *tail_got),
        width,
        n_ring * quarter,
        pltpu.VMEM((n_ring, hot_rows, FULL), F32),
        n_rep,
    )
    hot_got = [shift(hot_msg[k - 1], k, n_rep) for k in range(1, n_rep)]
    cold_own, *cold_msg = parts_call(
        cold_kernel,
        me,
        (wanted.reshape(1, n_table * HEAD_CAP), neg_ids, back),
        width,
        cold_rows // n_rep,
        pltpu.VMEM((n_table * HEAD_CAP, FULL), BF),
        n_rep,
    )
    cold_got = []
    for k in range(1, n_rep):
        cold_got.append(shift(cold_msg[k - 1], k, n_rep))
    hot_part = sum_call(hot_own, hot_got, (n_ring * quarter, FULL), F32)
    hot_rows_got = lax.all_to_all(
        hot_part.reshape(n_ring, quarter, FULL), "table", 0, 0, axis_index_groups=far
    )
    cold_part = sum_call(cold_own, cold_got, cold_got[0].shape, I16)
    cold_parts = [cold_part]
    for k in range(1, n_rep):
        cold_parts.append(shift(cold_part, k, n_rep))
    hot_sum = jnp.sum(hot_rows_got, axis=0)
    new_cold_table, new_cold_state = cold_update(me, cold_table, cold_state, cold_parts)

    hot_parts = [hot_sum]
    for k in range(1, n_rep):
        hot_parts.append(shift(hot_sum, k, n_rep))
    hot_total = jnp.zeros((n_rep, quarter, FULL), F32)
    for k, part in enumerate(hot_parts):
        hot_total = lax.dynamic_update_index_in_dim(
            hot_total, part, lax.rem(me[0] - k + n_rep, n_rep), 0
        )
    hot_total = narrow(hot_total.reshape(hot_rows, FULL), width)
    new_hot_table, new_hot_state = adagrad(hot_table, hot_state, hot_total)
    return (new_cold_table, new_cold_state, new_hot_table, new_hot_state)


def solution(mesh):
    in_specs = (
        P("table", None),
        P("table"),
        P("table", None),
        P("table"),
        P(),
        P(("rep", "table"), None),
        P(("rep", "table")),
        P(("rep", "table")),
        P(("rep", "table")),
        P("rep", "table"),
    )
    out_specs = (P("table", None), P("table"), P("table", None), P("table"))

    return jax.shard_map(
        per_device, mesh=mesh, in_specs=in_specs, out_specs=out_specs, check_vma=False
    )
```
